256 devices in a mesh: gx: 16 (over y, x), gy: 16 (over z, core).
Axes of the slice: x: 4, y: 4, z: 8, core: 2. Of those that a mesh axis runs over, the one named last changes fastest.
Arguments:
- velocity: float32 [3, 2, 2048, 2048], P(None, None, 'gx', 'gy'), may hold values from -8 to 8
- diffusion: float32 [2, 2048, 2048], P(None, 'gx', 'gy'), may hold values from 16384 to 262144
Outputs:
- new_velocity: float32 [3, 2, 2048, 2048], P(None, None, 'gx', 'gy')
The draws below stay inside these ranges and needn't reach their ends.
All inputs are finite; a program needn't handle non-finite values.
Results may differ from the reference program's by a relative error of at most 0.000024.
Values sent between devices are 32-bit elements; how exact they have to be, the bound alone decides.
No kernel may reach another device: no remote copies, remote signals or barrier semaphores. Data moves between devices by JAX's collectives and lax.ppermute only.
A program may use at most 64 MiB of HBM per device.

```python
import math
import jax
import jax.numpy as jnp
from jax import lax

PLANES = 2
NX = 2048
NY = 2048


def draw_velocity(key, part):
    keys = jax.random.split(jax.random.fold_in(key, 17), 4)
    waves_x = jax.random.randint(keys[0], (3, PLANES, 8), 1, 7).astype(jnp.float32)
    waves_y = jax.random.randint(keys[1], (3, PLANES, 8), 1, 7).astype(jnp.float32)
    phases = jax.random.uniform(keys[2], (2, 3, PLANES, 8), jnp.float32, 0.0, 6.2831853)
    coord_x = jnp.arange(NX, dtype=jnp.float32) / NX
    coord_y = jnp.arange(NY, dtype=jnp.float32) / NY
    along_x = jnp.cos(6.2831853 * waves_x[..., None] * coord_x + phases[0][..., None])
    along_y = jnp.cos(6.2831853 * waves_y[..., None] * coord_y + phases[1][..., None])
    smooth = 0.35 * jnp.einsum('cpkx,cpky->cpxy', along_x, along_y)
    rough = jnp.clip(0.5 * jax.random.normal(keys[3], (3, PLANES, NX, NY), jnp.float32), -3.0, 3.0)
    stream = 1.0
    mean_flow = jnp.array([stream, 0.0, 0.0], jnp.float32)[:, None, None, None]
    return (smooth + rough + mean_flow).astype(jnp.float32)


def level_of(key, shape, cuts, low, largest):
    gain, own = 1.0, jax.random.fold_in(key, 6)
    for position, shards_of in cuts:
        steps = jnp.exp(jax.random.uniform(jax.random.fold_in(own, position), (shards_of,), jnp.float32, low / len(cuts), largest / len(cuts)))
        gain = gain * jnp.repeat(steps, shape[position] // shards_of).reshape([-1 if axis == position else 1 for axis in range(len(shape))])
    return gain


def setup_inputs(seed: int = 0) -> dict:
    key_list = jax.random.split(jax.random.key(seed), 3)
    return {
        "velocity": draw_velocity(jax.random.fold_in(key_list[2], 71), 0),
        "diffusion": jnp.clip(jnp.exp(math.log(262144.0) - 2.7725887 * jax.random.uniform(key_list[1], (PLANES, NX, NY), jnp.float32) ** level_of(key_list[1], (PLANES, NX, NY), ((1, 16), (2, 16)), -0.2, 0.2)), 16384.0, 262144.0),
    }


courant = 0.25


def thomas(source, lower_face, upper_face, cell_dim):
    source_t = jnp.moveaxis(source, cell_dim, 0)
    lower_t = jnp.moveaxis(lower_face, cell_dim - 1, 0)
    upper_t = jnp.moveaxis(upper_face, cell_dim - 1, 0)

    def downward(state, entries):
        share_prev, value_prev = state
        low_now, high_now, src_now = entries
        denom = 1.0 + high_now + low_now * share_prev
        share_next = (1.0 + low_now * share_prev) / denom
        value_next = (src_now + low_now * value_prev) / denom
        return (share_next, value_next), (share_next, value_next)

    start = (jnp.ones(lower_t.shape[1:], jnp.float32), jnp.zeros(source_t.shape[1:], jnp.float32))
    unused, (share_all, value_all) = lax.scan(downward, start, (lower_t, upper_t, source_t))

    def upward(w_next, entries):
        share_now, value_now = entries
        w_now = value_now + (1.0 - share_now) * w_next
        return w_now, w_now

    unused_two, w_all = lax.scan(upward, jnp.zeros(source_t.shape[1:], jnp.float32), (share_all, value_all), reverse=True)
    return jnp.moveaxis(w_all, 0, cell_dim)


def reference(velocity, diffusion):
    padded = jnp.pad(velocity, ((0, 0), (0, 0), (1, 1), (1, 1)))
    grad_x = padded[:, :, 2:, 1:-1] - padded[:, :, :-2, 1:-1]
    grad_y = padded[:, :, 1:-1, 2:] - padded[:, :, 1:-1, :-2]
    source = velocity - (0.5 * courant) * (velocity[0] * grad_x + velocity[1] * grad_y)
    viscous = jnp.pad(diffusion, ((0, 0), (1, 1), (1, 1)))
    lower_x = 0.5 * (viscous[:, :-2, 1:-1] + diffusion)
    upper_x = 0.5 * (viscous[:, 2:, 1:-1] + diffusion)
    lower_y = 0.5 * (viscous[:, 1:-1, :-2] + diffusion)
    upper_y = 0.5 * (viscous[:, 1:-1, 2:] + diffusion)
    middle = thomas(source, lower_x, upper_x, 2)
    return thomas(middle, lower_y, upper_y, 3)
```

```python
import jax
import jax.numpy as jnp
from jax import lax
from jax.experimental import pallas as pl
from jax.experimental.pallas import tpu as pltpu
from jax.sharding import PartitionSpec as P


COURANT = 0.25
HALF = 0.5 * COURANT
SEG = 16
PLANES = 2
COMPS = 3
LANES = 128
ROWS_X = 40
ROWS_Y = 24
ROW_G, ROW_EL, ROW_ER, ROW_DHI, ROW_DLO = 0, 2, 4, 6, 8
ROW_JL, ROW_JR, ROW_VLO, ROW_VHI = 10, 16, 22, 28

f32 = jnp.float32
VMEM = pltpu.VMEM


def sub_iota():
    return lax.broadcasted_iota(jnp.int32, (8, LANES), 0)


def lane_iota():
    return lax.broadcasted_iota(jnp.int32, (8, LANES), 1)


def ahead(x, count):
    return pltpu.roll(x, 8 - count, 0)


def after(x, count):
    return pltpu.roll(x, count, 0)


def strided(ref, lead, t):
    return ref[lead, pl.ds(t, 8, stride=SEG), :]


def factor(cells, first, coef_ref, tree_ref, head_ref, plane):
    row = sub_iota()
    last = row == 7
    faces = [0.5 * (cells[t] + cells[t + 1]) for t in range(SEG - 1)]
    faces.append(0.5 * (cells[SEG - 1] + ahead(cells[0], 1)))
    leak_l = 1.0 + jnp.where(jnp.logical_and(row == 0, first), 0.5 * cells[0], 0.0)
    g = faces[0]
    leak_r = jnp.ones_like(g)
    for t in range(1, SEG):
        f = faces[t]
        inv = 1.0 / (g + f + leak_r)
        a = g * inv
        b = f * inv
        if t == SEG - 1:
            inv = jnp.where(last, 0.0, inv)
            g = jnp.where(last, g, a * f)
            a = jnp.where(last, 0.0, a)
            b = jnp.where(last, 1.0, b)
            leak_l = leak_l + a * leak_r
            leak_r = b * leak_r
        else:
            g = a * f
            leak_l = leak_l + a * leak_r
            leak_r = 1.0 + b * leak_r
        coef_ref[plane, 0, t] = a
        coef_ref[plane, 1, t] = b
        coef_ref[plane, 2, t] = inv
    for level in range(3):
        count = 1 << level
        g_next = ahead(g, count)
        leak = leak_r + ahead(leak_l, count)
        inv = 1.0 / (g + g_next + leak)
        a = g * inv
        b = g_next * inv
        g = a * g_next
        leak_l = leak_l + a * leak
        leak_r = ahead(leak_r, count) + b * leak
        tree_ref[plane, level, 0] = a
        tree_ref[plane, level, 1] = b
        tree_ref[plane, level, 2] = inv
    for base, value in ((ROW_G, g), (ROW_EL, leak_l), (ROW_ER, leak_r)):
        head_ref[base + plane : base + plane + 1, :] = value[0:1]
    head_ref[ROW_DHI + plane : ROW_DHI + plane + 1, :] = cells[SEG - 1][7:8]
    head_ref[ROW_DLO + plane : ROW_DLO + plane + 1, :] = cells[0][0:1]


def condense(sources, coef_ref, tree_ref, q_ref, qtree_ref, plane, comp):
    k = comp * PLANES + plane
    left = sources[0]
    right = sources[1]
    for t in range(1, SEG):
        q_ref[k, t] = coef_ref[plane, 2, t] * right
        left = left + coef_ref[plane, 0, t] * right
        right = coef_ref[plane, 1, t] * right
        if t < SEG - 1:
            right = right + sources[t + 1]
    for level in range(3):
        count = 1 << level
        j = right + ahead(left, count)
        left = left + tree_ref[plane, level, 0] * j
        right = ahead(right, count) + tree_ref[plane, level, 1] * j
        qtree_ref[k, level] = tree_ref[plane, level, 2] * j
    return left, right


def unfold(low, high, coef_ref, tree_ref, q_ref, qtree_ref, plane, comp, store):
    k = comp * PLANES + plane
    row = sub_iota()

    def mid(level, lo, hi):
        return (
            tree_ref[plane, level, 0] * lo
            + tree_ref[plane, level, 1] * hi
            + qtree_ref[k, level]
        )

    for level in (2, 1, 0):
        count = 1 << level
        between = mid(level, low, high)
        late = (row & count) != 0
        low = jnp.where(late, after(between, count), low)
        high = jnp.where(late, after(high, count), between)
    store(0, low)
    cell = high
    for t in range(SEG - 1, 0, -1):
        cell = (
            coef_ref[plane, 0, t] * low
            + q_ref[k, t]
            + coef_ref[plane, 1, t] * cell
        )
        store(t, cell)


def solve_ends(ring_ref, rows, me, count, plane, advect):
    row = sub_iota()

    def take(which, half, shift=0):
        slot = me + 8 * half + shift
        return ring_ref[pl.ds(slot * rows + which + plane, 8, stride=rows), :]

    halves = []
    for half in (0, 1):
        place = (me + 8 * half + row) & (count - 1)
        wall = place == count - 1
        g = take(ROW_G, half)
        leak_l = take(ROW_EL, half)
        leak_r = take(ROW_ER, half)
        f = 0.5 * (take(ROW_DHI, half) + jnp.where(wall, 0.0, take(ROW_DLO, half, 1)))
        inv = 1.0 / (g + f + leak_r)
        a = g * inv
        b = f * inv
        through = a * f
        leak_l = leak_l + a * leak_r
        leak_l = jnp.where(wall, leak_l + through, leak_l)
        own = (a, b, inv)
        g = jnp.where(wall, 0.0, through)
        leak_r = jnp.where(wall, 0.0, b * leak_r)
        b_cut = jnp.where(wall, 0.0, b)
        currents = []
        if advect:
            up_lo = jnp.where(place == 0, 0.0, HALF * take(ROW_VLO, half))
            up_hi = jnp.where(wall, 0.0, HALF * take(ROW_VHI, half))
        for comp in range(COMPS):
            left = take(ROW_JL + comp * PLANES, half)
            right = take(ROW_JR + comp * PLANES, half)
            if advect:
                same = after(take(ROW_VHI + comp * PLANES, half), 1)
                other = after(take(ROW_VHI + comp * PLANES, 1 - half), 1)
                left = left + up_lo * jnp.where(row == 0, other, same)
                right = right - up_hi * take(ROW_VLO + comp * PLANES, half, 1)
            q = inv * right
            left = left + a * right
            currents.append((left, b_cut * right, q))
        levels = []
        for level in range(3):
            step = 1 << level
            g_next = ahead(g, step)
            leak = leak_r + ahead(leak_l, step)
            inv_n = 1.0 / (g + g_next + leak)
            a_n = g * inv_n
            b_n = g_next * inv_n
            g = a_n * g_next
            leak_l = leak_l + a_n * leak
            leak_r = ahead(leak_r, step) + b_n * leak
            levels.append((a_n, b_n, inv_n))
        merged = []
        for left, right, q in currents:
            terms = []
            for level in range(3):
                step = 1 << level
                a_n, b_n, inv_n = levels[level]
                j = right + ahead(left, step)
                left = left + a_n * j
                right = ahead(right, step) + b_n * j
                terms.append(inv_n * j)
            merged.append((left, right, q, terms))
        halves.append((own, g, leak_l, leak_r, levels, merged))
    own, g, leak_l, leak_r, levels, merged = halves[0]
    _, g_next, leak_l_next, leak_r_next, _, merged_next = halves[1]
    leak = leak_r + leak_l_next
    inv = 1.0 / (g + g_next + leak)
    a = g * inv
    b = g_next * inv
    total = 1.0 / (leak_l + a * leak + leak_r_next + b * leak)
    at_wall = me == count - 1
    ends = []
    for comp in range(COMPS):
        left, right, q, terms = merged[comp]
        left_next, right_next, _, _ = merged_next[comp]
        j = right + left_next
        first = (left + a * j + right_next + b * j) * total
        high = (a + b) * first + inv * j
        for level in (2, 1, 0):
            a_n, b_n, _ = levels[level]
            high = a_n * first + b_n * high + terms[level]
        high = jnp.where(at_wall, 0.0, high)
        ends.append((first, own[0] * first + own[1] * high + q))
    return ends


def fill_ring(got_ref, ring_ref, rows, count):
    size = rows * count
    block = got_ref[...]
    ring_ref[0:size, :] = block
    ring_ref[size : 2 * size, :] = block


def send_all(page_ref, out_ref, rows, count):
    page = page_ref[...]
    for i in range(count):
        out_ref[i * rows : (i + 1) * rows, :] = page


def edges_kernel(velocity_ref, low_ref, high_ref):
    for k in range(COMPS * PLANES):
        comp, plane = divmod(k, PLANES)
        turned = jnp.transpose(velocity_ref[comp, plane])
        low_ref[k : k + 1, :] = turned[0:1]
        high_ref[k : k + 1, :] = turned[LANES - 1 : LANES]
    low_ref[6:8, :] = jnp.zeros((2, LANES), f32)
    high_ref[6:8, :] = jnp.zeros((2, LANES), f32)


def matrix_kernel(diffusion_ref, cx_ref, tx_ref, hx_ref, cy_ref, ty_ref, hy_ref, turn_ref):
    first_x = lax.axis_index("gx") == 0
    first_y = lax.axis_index("gy") == 0
    for plane in range(PLANES):
        turn_ref[plane] = jnp.transpose(diffusion_ref[plane])
        cells = [strided(diffusion_ref, plane, t) for t in range(SEG)]
        factor(cells, first_x, cx_ref, tx_ref, hx_ref, plane)
        cells = [strided(turn_ref, plane, t) for t in range(SEG)]
        factor(cells, first_y, cy_ref, ty_ref, hy_ref, plane)
    for ref in (hx_ref, hy_ref):
        ref[10:16, :] = jnp.zeros((6, LANES), f32)


def source_kernel(count, velocity_ref, from_low_ref, from_high_ref, coef_ref, tree_ref, head_ref,
                  out_ref, q_ref, qtree_ref, edge_ref, halo_ref, page_ref):
    me_y = lax.axis_index("gy")
    count_y = lax.axis_size("gy")
    row = sub_iota()
    lane = lane_iota()
    low = jnp.where(me_y == 0, 0.0, from_low_ref[...])
    high = jnp.where(me_y == count_y - 1, 0.0, from_high_ref[...])
    edge_ref[0:8, :] = low
    edge_ref[8:16, :] = high
    edge_ref[16:, :] = jnp.zeros((LANES - 16, LANES), f32)
    halo_ref[...] = jnp.transpose(edge_ref[...])
    page_ref[0:16, :] = head_ref[...]
    page_ref[32:, :] = jnp.zeros((ROWS_X - 32, LANES), f32)
    for plane in range(PLANES):
        cells = [
            [velocity_ref[comp, plane, pl.ds(t, 8, stride=SEG), :] for t in range(SEG)]
            for comp in range(COMPS)
        ]
        halos = [halo_ref[pl.ds(t, 8, stride=SEG), :] for t in range(SEG)]
        for comp in range(COMPS):
            k = comp * PLANES + plane
            own = cells[comp]
            sources = []
            for t in range(SEG):
                if t < SEG - 1:
                    fore = own[t + 1]
                else:
                    fore = jnp.where(row == 7, 0.0, ahead(own[0], 1))
                if t > 0:
                    back = own[t - 1]
                else:
                    back = jnp.where(row == 0, 0.0, after(own[SEG - 1], 1))
                lo = jnp.broadcast_to(halos[t][:, k : k + 1], (8, LANES))
                hi = jnp.broadcast_to(halos[t][:, 8 + k : 9 + k], (8, LANES))
                right = jnp.where(lane == LANES - 1, hi, pltpu.roll(own[t], LANES - 1, 1))
                left = jnp.where(lane == 0, lo, pltpu.roll(own[t], 1, 1))
                sources.append(
                    own[t]
                    - HALF * (cells[0][t] * (fore - back) + cells[1][t] * (right - left))
                )
            left, right = condense(sources, coef_ref, tree_ref, q_ref, qtree_ref, plane, comp)
            page_ref[ROW_JL + k : ROW_JL + k + 1, :] = left[0:1]
            page_ref[ROW_JR + k : ROW_JR + k + 1, :] = right[0:1]
            page_ref[ROW_VLO + k : ROW_VLO + k + 1, :] = own[0][0:1]
            page_ref[ROW_VHI + k : ROW_VHI + k + 1, :] = own[SEG - 1][7:8]
    send_all(page_ref, out_ref, ROWS_X, count)


def middle_kernel(count_x, count_y, got_ref, cx_ref, tx_ref, qx_ref, qtx_ref, cy_ref, ty_ref, hy_ref,
                  out_ref, q_ref, qtree_ref, ring_ref, plane_ref, turn_ref, page_ref):
    me = lax.axis_index("gx")
    fill_ring(got_ref, ring_ref, ROWS_X, count_x)
    page_ref[0:16, :] = hy_ref[...]
    page_ref[16:, :] = jnp.zeros((ROWS_Y - 16, LANES), f32)
    for plane in range(PLANES):
        ends = solve_ends(ring_ref, ROWS_X, me, count_x, plane, True)
        for comp in range(COMPS):
            k = comp * PLANES + plane
            low, high = ends[comp]

            def store(t, value):
                plane_ref[k, pl.ds(t, 8, stride=SEG), :] = value

            unfold(low, high, cx_ref, tx_ref, qx_ref, qtx_ref, plane, comp, store)
            turn_ref[k] = jnp.transpose(plane_ref[k])
            sources = [strided(turn_ref, k, t) for t in range(SEG)]
            left, right = condense(sources, cy_ref, ty_ref, q_ref, qtree_ref, plane, comp)
            page_ref[ROW_JL + k : ROW_JL + k + 1, :] = left[0:1]
            page_ref[ROW_JR + k : ROW_JR + k + 1, :] = right[0:1]
    send_all(page_ref, out_ref, ROWS_Y, count_y)


def final_kernel(count, got_ref, coef_ref, tree_ref, q_ref, qtree_ref, out_ref, ring_ref, plane_ref):
    me = lax.axis_index("gy")
    fill_ring(got_ref, ring_ref, ROWS_Y, count)
    for plane in range(PLANES):
        ends = solve_ends(ring_ref, ROWS_Y, me, count, plane, False)
        for comp in range(COMPS):
            k = comp * PLANES + plane
            low, high = ends[comp]

            def store(t, value):
                plane_ref[k, pl.ds(t, 8, stride=SEG), :] = value

            unfold(low, high, coef_ref, tree_ref, q_ref, qtree_ref, plane, comp, store)
            out_ref[comp, plane] = jnp.transpose(plane_ref[k])


def shape(*dims):
    return jax.ShapeDtypeStruct(dims, f32)


def call(kernel, outs, scratch, cost, *args):
    spec = pl.BlockSpec(memory_space=VMEM)
    return pl.pallas_call(
        kernel,
        out_shape=outs,
        in_specs=[spec] * len(args),
        out_specs=jax.tree.map(lambda _: spec, outs),
        scratch_shapes=scratch,
        cost_estimate=pl.CostEstimate(flops=cost, bytes_accessed=1 << 19, transcendentals=0),
        compiler_params=pltpu.CompilerParams(vmem_limit_bytes=8 << 20),
    )(*args)


def local(velocity, diffusion):
    from functools import partial

    count_x = lax.axis_size("gx")
    count_y = lax.axis_size("gy")
    tile = (8, LANES)
    n = COMPS * PLANES
    low, high = call(edges_kernel, (shape(*tile), shape(*tile)), [], 1 << 17, velocity)
    from_low = lax.ppermute(high, "gy", [(i, (i + 1) % count_y) for i in range(count_y)])
    from_high = lax.ppermute(low, "gy", [((i + 1) % count_y, i) for i in range(count_y)])
    coef = shape(PLANES, 3, SEG, *tile)
    tree = shape(PLANES, 3, 3, *tile)
    head = shape(16, LANES)
    q_all = shape(n, SEG, *tile)
    q_tree = shape(n, 3, *tile)
    block = VMEM((n, LANES, LANES), f32)
    cx, tx, hx, cy, ty, hy = call(
        matrix_kernel,
        (coef, tree, head, coef, tree, head),
        [VMEM((PLANES, LANES, LANES), f32)],
        1 << 21,
        diffusion,
    )
    sent, qx, qtx = call(
        partial(source_kernel, count_x),
        (shape(count_x * ROWS_X, LANES), q_all, q_tree),
        [VMEM((LANES, LANES), f32), VMEM((LANES, LANES), f32), VMEM((ROWS_X, LANES), f32)],
        1 << 22,
        velocity, from_low, from_high, cx, tx, hx,
    )
    got = lax.all_to_all(sent.reshape(count_x, ROWS_X, LANES), "gx", 0, 0)
    sent, qy, qty = call(
        partial(middle_kernel, count_x, count_y),
        (shape(count_y * ROWS_Y, LANES), q_all, q_tree),
        [VMEM((2 * count_x * ROWS_X, LANES), f32), block, block, VMEM((ROWS_Y, LANES), f32)],
        1 << 22,
        got.reshape(-1, LANES), cx, tx, qx, qtx, cy, ty, hy,
    )
    got = lax.all_to_all(sent.reshape(count_y, ROWS_Y, LANES), "gy", 0, 0)
    return call(
        partial(final_kernel, count_y),
        shape(COMPS, PLANES, LANES, LANES),
        [VMEM((2 * count_y * ROWS_Y, LANES), f32), block],
        1 << 22,
        got.reshape(-1, LANES), cy, ty, qy, qty,
    )


def solution(mesh):
    in_specs = (P(None, None, "gx", "gy"), P(None, "gx", "gy"))
    out_specs = P(None, None, "gx", "gy")
    return jax.shard_map(local, mesh=mesh, in_specs=in_specs, out_specs=out_specs, check_vma=False)
```

```python
from functools import partial

import jax
import jax.numpy as jnp
from jax import lax
from jax.experimental import pallas as pl
from jax.experimental.pallas import tpu as pltpu
from jax.sharding import PartitionSpec as P


COURANT = 0.25
HALF = 0.5 * COURANT
SEG = 16
PLANES = 2
COMPS = 3
LANES = 128
ROWS_X = 40
ROWS_Y = 24
ROW_G, ROW_EL, ROW_ER, ROW_DHI, ROW_DLO = 0, 2, 4, 6, 8
ROW_JL, ROW_JR, ROW_VLO, ROW_VHI = 10, 16, 22, 28
Y_JL, Y_JR, ROWS_SENT_Y = 6, 12, 18
OWN_A, OWN_B, OWN_Q = 0, 2, 4

f32 = jnp.float32
VMEM = pltpu.VMEM
HBM = pltpu.HBM


def sub_iota():
    return lax.broadcasted_iota(jnp.int32, (8, LANES), 0)


def lane_iota():
    return lax.broadcasted_iota(jnp.int32, (8, LANES), 1)


def ahead(x, count):
    return pltpu.roll(x, 8 - count, 0)


def after(x, count):
    return pltpu.roll(x, count, 0)


def strided(ref, lead, t):
    return ref[lead, pl.ds(t, 8, stride=SEG), :]


def factor(cells, first, coef_ref, tree_ref, head_ref, plane):
    row = sub_iota()
    last = row == 7
    faces = [0.5 * (cells[t] + cells[t + 1]) for t in range(SEG - 1)]
    faces.append(0.5 * (cells[SEG - 1] + ahead(cells[0], 1)))
    leak_l = 1.0 + jnp.where(jnp.logical_and(row == 0, first), 0.5 * cells[0], 0.0)
    g = faces[0]
    leak_r = jnp.ones_like(g)
    for t in range(1, SEG):
        f = faces[t]
        inv = 1.0 / (g + f + leak_r)
        a = g * inv
        b = f * inv
        if t == SEG - 1:
            inv = jnp.where(last, 0.0, inv)
            g = jnp.where(last, g, a * f)
            a = jnp.where(last, 0.0, a)
            b = jnp.where(last, 1.0, b)
            leak_l = leak_l + a * leak_r
            leak_r = b * leak_r
        else:
            g = a * f
            leak_l = leak_l + a * leak_r
            leak_r = 1.0 + b * leak_r
        coef_ref[plane, 0, t] = a
        coef_ref[plane, 1, t] = b
        coef_ref[plane, 2, t] = inv
    for level in range(3):
        count = 1 << level
        g_next = ahead(g, count)
        leak = leak_r + ahead(leak_l, count)
        inv = 1.0 / (g + g_next + leak)
        a = g * inv
        b = g_next * inv
        g = a * g_next
        leak_l = leak_l + a * leak
        leak_r = ahead(leak_r, count) + b * leak
        tree_ref[plane, level, 0] = a
        tree_ref[plane, level, 1] = b
        tree_ref[plane, level, 2] = inv
    for base, value in ((ROW_G, g), (ROW_EL, leak_l), (ROW_ER, leak_r)):
        head_ref[base + plane : base + plane + 1, :] = value[0:1]
    head_ref[ROW_DHI + plane : ROW_DHI + plane + 1, :] = cells[SEG - 1][7:8]
    head_ref[ROW_DLO + plane : ROW_DLO + plane + 1, :] = cells[0][0:1]


def condense(sources, coef_ref, tree_ref, q_ref, qtree_ref, plane, comp):
    k = comp * PLANES + plane
    left = sources[0]
    right = sources[1]
    for t in range(1, SEG):
        q_ref[k, t] = coef_ref[plane, 2, t] * right
        left = left + coef_ref[plane, 0, t] * right
        right = coef_ref[plane, 1, t] * right
        if t < SEG - 1:
            right = right + sources[t + 1]
    for level in range(3):
        count = 1 << level
        j = right + ahead(left, count)
        left = left + tree_ref[plane, level, 0] * j
        right = ahead(right, count) + tree_ref[plane, level, 1] * j
        qtree_ref[k, level] = tree_ref[plane, level, 2] * j
    return left, right


def unfold(low, high, coef_ref, tree_ref, q_ref, qtree_ref, plane, comp, store):
    k = comp * PLANES + plane
    row = sub_iota()

    def mid(level, lo, hi):
        return (
            tree_ref[plane, level, 0] * lo
            + tree_ref[plane, level, 1] * hi
            + qtree_ref[k, level]
        )

    for level in (2, 1, 0):
        count = 1 << level
        between = mid(level, low, high)
        late = (row & count) != 0
        low = jnp.where(late, after(between, count), low)
        high = jnp.where(late, after(high, count), between)
    store(0, low)
    cell = high
    for t in range(SEG - 1, 0, -1):
        cell = (
            coef_ref[plane, 0, t] * low
            + q_ref[k, t]
            + coef_ref[plane, 1, t] * cell
        )
        store(t, cell)


def cyclic(me, half, count):
    return (me + 8 * half + sub_iota()) & (count - 1)


def solve_ring(blocks, me, count):
    halves = []
    for g, leak_l, leak_r, currents in blocks:
        levels = []
        for level in range(3):
            step = 1 << level
            g_next = ahead(g, step)
            leak = leak_r + ahead(leak_l, step)
            inv = 1.0 / (g + g_next + leak)
            a = g * inv
            b = g_next * inv
            g = a * g_next
            leak_l = leak_l + a * leak
            leak_r = ahead(leak_r, step) + b * leak
            levels.append((a, b, inv))
        merged = []
        for left, right in currents:
            terms = []
            for level in range(3):
                step = 1 << level
                a, b, inv = levels[level]
                j = right + ahead(left, step)
                left = left + a * j
                right = ahead(right, step) + b * j
                terms.append(inv * j)
            merged.append((left, right, terms))
        halves.append((g, leak_l, leak_r, levels, merged))
    g, leak_l, leak_r, levels, merged = halves[0]
    g_next, leak_l_next, leak_r_next, _, merged_next = halves[1]
    leak = leak_r + leak_l_next
    inv = 1.0 / (g + g_next + leak)
    a = g * inv
    b = g_next * inv
    total = 1.0 / (leak_l + a * leak + leak_r_next + b * leak)
    ends = []
    for comp in range(COMPS):
        left, right, terms = merged[comp]
        left_next, right_next, _ = merged_next[comp]
        j = right + left_next
        first = (left + a * j + right_next + b * j) * total
        high = (a + b) * first + inv * j
        for level in (2, 1, 0):
            high = levels[level][0] * first + levels[level][1] * high + terms[level]
        ends.append((first, jnp.where(me == count - 1, 0.0, high)))
    return ends


def solve_x(ring_ref, me, count, plane):
    row = sub_iota()

    def take(which, half):
        return ring_ref[pl.ds(8 * half * ROWS_X + which + plane, 8, stride=ROWS_X), :]

    def both(which):
        return take(which, 0), take(which, 1)

    def before(pair, half):
        return jnp.where(row == 0, after(pair[1 - half], 1), after(pair[half], 1))

    def beyond(pair, half):
        return jnp.where(row == 7, ahead(pair[1 - half], 1), ahead(pair[half], 1))

    first_faces = both(ROW_DLO)
    low_cells = [both(ROW_VLO + comp * PLANES) for comp in range(COMPS)]
    high_cells = [both(ROW_VHI + comp * PLANES) for comp in range(COMPS)]
    blocks = []
    own = None
    for half in (0, 1):
        place = cyclic(me, half, count)
        wall = place == count - 1
        g = take(ROW_G, half)
        leak_l = take(ROW_EL, half)
        leak_r = take(ROW_ER, half)
        f = 0.5 * (take(ROW_DHI, half) + jnp.where(wall, 0.0, beyond(first_faces, half)))
        inv = 1.0 / (g + f + leak_r)
        a = g * inv
        b = f * inv
        through = a * f
        leak_l = leak_l + a * leak_r
        leak_l = jnp.where(wall, leak_l + through, leak_l)
        up_lo = jnp.where(place == 0, 0.0, HALF * low_cells[0][half])
        up_hi = jnp.where(wall, 0.0, HALF * high_cells[0][half])
        b_cut = jnp.where(wall, 0.0, b)
        currents = []
        terms = []
        for comp in range(COMPS):
            left = take(ROW_JL + comp * PLANES, half)
            right = take(ROW_JR + comp * PLANES, half)
            left = left + up_lo * before(high_cells[comp], half)
            right = right - up_hi * beyond(low_cells[comp], half)
            terms.append(inv * right)
            currents.append((left + a * right, b_cut * right))
        if half == 0:
            own = (a, b, terms)
        blocks.append((jnp.where(wall, 0.0, through), leak_l, b_cut * leak_r, currents))
    ends = solve_ring(blocks, me, count)
    a, b, terms = own
    return [
        (first, a * first + b * high + terms[comp]) for comp, (first, high) in enumerate(ends)
    ]


def solve_y(ring_ref, own_ref, me, count, plane):
    def take(which, half):
        return ring_ref[pl.ds(8 * half * ROWS_Y + which + plane, 8, stride=ROWS_Y), :]

    def own(which):
        return own_ref[which + plane : which + plane + 1, :]

    blocks = [
        (
            take(ROW_G, half),
            take(ROW_EL, half),
            take(ROW_ER, half),
            [
                (take(Y_JL + comp * PLANES, half), take(Y_JR + comp * PLANES, half))
                for comp in range(COMPS)
            ],
        )
        for half in (0, 1)
    ]
    ends = solve_ring(blocks, me, count)
    return [
        (first, own(OWN_A) * first + own(OWN_B) * high + own(OWN_Q + comp * PLANES))
        for comp, (first, high) in enumerate(ends)
    ]


def edges_kernel(velocity_ref, diffusion_ref, low_ref, high_ref, v_ref, d_ref, turn_ref, sem):
    copies = [
        pltpu.make_async_copy(velocity_ref, v_ref, sem.at[0]),
        pltpu.make_async_copy(diffusion_ref, d_ref, sem.at[1]),
    ]
    for copy in copies:
        copy.start()
    for copy in copies:
        copy.wait()
    for k in range(COMPS * PLANES + PLANES):
        if k < COMPS * PLANES:
            comp, plane = divmod(k, PLANES)
            turned = jnp.transpose(v_ref[comp, plane])
        else:
            turned = jnp.transpose(d_ref[k - 6])
            turn_ref[k - 6] = turned
        low_ref[k : k + 1, :] = turned[0:1]
        high_ref[k : k + 1, :] = turned[LANES - 1 : LANES]


def matrix_kernel(diffusion_ref, turn_ref, cx_ref, tx_ref, hx_ref, cy_ref, ty_ref, hy_ref):
    first_x = lax.axis_index("gx") == 0
    first_y = lax.axis_index("gy") == 0
    for plane in range(PLANES):
        cells = [strided(diffusion_ref, plane, t) for t in range(SEG)]
        factor(cells, first_x, cx_ref, tx_ref, hx_ref, plane)
        cells = [strided(turn_ref, plane, t) for t in range(SEG)]
        factor(cells, first_y, cy_ref, ty_ref, hy_ref, plane)
    for ref in (hx_ref, hy_ref):
        ref[10:16, :] = jnp.zeros((6, LANES), f32)


def source_kernel(count, velocity_ref, from_low_ref, from_high_ref, coef_ref, tree_ref, head_ref,
                  out_ref, q_ref, qtree_ref, edge_ref, halo_ref, page_ref):
    me_y = lax.axis_index("gy")
    count_y = lax.axis_size("gy")
    row = sub_iota()
    lane = lane_iota()
    low = jnp.where(me_y == 0, 0.0, from_low_ref[...])
    high = jnp.where(me_y == count_y - 1, 0.0, from_high_ref[...])
    edge_ref[0:8, :] = low
    edge_ref[8:16, :] = high
    edge_ref[16:, :] = jnp.zeros((LANES - 16, LANES), f32)
    halo_ref[...] = jnp.transpose(edge_ref[...])
    page_ref[0:16, :] = head_ref[...]
    page_ref[32:, :] = jnp.zeros((ROWS_X - 32, LANES), f32)
    for plane in range(PLANES):
        cells = [
            [velocity_ref[comp, plane, pl.ds(t, 8, stride=SEG), :] for t in range(SEG)]
            for comp in range(COMPS)
        ]
        halos = [halo_ref[pl.ds(t, 8, stride=SEG), :] for t in range(SEG)]
        for comp in range(COMPS):
            k = comp * PLANES + plane
            own = cells[comp]
            sources = []
            for t in range(SEG):
                if t < SEG - 1:
                    fore = own[t + 1]
                else:
                    fore = jnp.where(row == 7, 0.0, ahead(own[0], 1))
                if t > 0:
                    back = own[t - 1]
                else:
                    back = jnp.where(row == 0, 0.0, after(own[SEG - 1], 1))
                lo = jnp.broadcast_to(halos[t][:, k : k + 1], (8, LANES))
                hi = jnp.broadcast_to(halos[t][:, 8 + k : 9 + k], (8, LANES))
                right = jnp.where(lane == LANES - 1, hi, pltpu.roll(own[t], LANES - 1, 1))
                left = jnp.where(lane == 0, lo, pltpu.roll(own[t], 1, 1))
                sources.append(
                    own[t]
                    - HALF * (cells[0][t] * (fore - back) + cells[1][t] * (right - left))
                )
            left, right = condense(sources, coef_ref, tree_ref, q_ref, qtree_ref, plane, comp)
            page_ref[ROW_JL + k : ROW_JL + k + 1, :] = left[0:1]
            page_ref[ROW_JR + k : ROW_JR + k + 1, :] = right[0:1]
            page_ref[ROW_VLO + k : ROW_VLO + k + 1, :] = own[0][0:1]
            page_ref[ROW_VHI + k : ROW_VHI + k + 1, :] = own[SEG - 1][7:8]
    page = page_ref[...]
    for i in range(count):
        out_ref[i] = page


def middle_kernel(count_x, count_y, got_ref, from_high_ref, cx_ref, tx_ref, qx_ref, qtx_ref, cy_ref,
                  ty_ref, hy_ref, out_ref, q_ref, qtree_ref, own_ref, ring_ref, plane_ref, turn_ref):
    me = lax.axis_index("gx")
    wall = lax.axis_index("gy") == count_y - 1
    for i in range(count_x):
        slot = (i - me + count_x) & (count_x - 1)
        ring_ref[pl.ds(pl.multiple_of(slot * ROWS_X, 8), ROWS_X), :] = got_ref[i]
    own_ref[10:16, :] = jnp.zeros((6, LANES), f32)
    values = {}
    for plane in range(PLANES):

        def head(which):
            return hy_ref[which + plane : which + plane + 1, :]

        g = head(ROW_G)
        leak_r = head(ROW_ER)
        beyond = from_high_ref[6 + plane : 7 + plane, :]
        f = 0.5 * (head(ROW_DHI) + jnp.where(wall, 0.0, beyond))
        inv = 1.0 / (g + f + leak_r)
        a = g * inv
        b = f * inv
        through = a * f
        b_cut = jnp.where(wall, 0.0, b)
        own_ref[OWN_A + plane : OWN_A + plane + 1, :] = a
        own_ref[OWN_B + plane : OWN_B + plane + 1, :] = b
        values[ROW_G + plane] = jnp.where(wall, 0.0, through)
        leak_l = head(ROW_EL) + a * leak_r
        values[ROW_EL + plane] = jnp.where(wall, leak_l + through, leak_l)
        values[ROW_ER + plane] = b_cut * leak_r
        ends = solve_x(ring_ref, me, count_x, plane)
        for comp in range(COMPS):
            k = comp * PLANES + plane
            low, high = ends[comp]

            def store(t, value):
                plane_ref[k, pl.ds(t, 8, stride=SEG), :] = value

            unfold(low, high, cx_ref, tx_ref, qx_ref, qtx_ref, plane, comp, store)
            turn_ref[k] = jnp.transpose(plane_ref[k])
            sources = [strided(turn_ref, k, t) for t in range(SEG)]
            left, right = condense(sources, cy_ref, ty_ref, q_ref, qtree_ref, plane, comp)
            right = right[0:1]
            own_ref[OWN_Q + k : OWN_Q + k + 1, :] = inv * right
            values[Y_JL + k] = left[0:1] + a * right
            values[Y_JR + k] = b_cut * right
    for pair in range(ROWS_SENT_Y // 2):
        rows = jnp.concatenate([values[2 * pair], values[2 * pair + 1]], 0)
        for i in range(count_y):
            out_ref[i, pair] = rows


def final_kernel(count, got_ref, own_ref, coef_ref, tree_ref, q_ref, qtree_ref, out_ref, ring_ref,
                 plane_ref, turn_ref, sem):
    me = lax.axis_index("gy")
    for i in range(count):
        slot = (i - me + count) & (count - 1)
        base = slot * ROWS_Y
        for pair in range(ROWS_SENT_Y // 2):
            ring_ref[pl.ds(base + 2 * pair, 2), :] = got_ref[i, pair]
    copies = []
    for plane in range(PLANES):
        ends = solve_y(ring_ref, own_ref, me, count, plane)
        for comp in range(COMPS):
            k = comp * PLANES + plane
            low, high = ends[comp]

            def store(t, value):
                plane_ref[k, pl.ds(t, 8, stride=SEG), :] = value

            unfold(low, high, coef_ref, tree_ref, q_ref, qtree_ref, plane, comp, store)
            turn_ref[k] = jnp.transpose(plane_ref[k])
            copy = pltpu.make_async_copy(turn_ref.at[k], out_ref.at[comp, plane], sem.at[k])
            copy.start()
            copies.append(copy)
    for copy in copies:
        copy.wait()


def shape(*dims):
    return jax.ShapeDtypeStruct(dims, f32)


def call(kernel, ins, outs, scratch, cost, *args):
    return pl.pallas_call(
        kernel,
        out_shape=tuple(o for o, _ in outs),
        in_specs=[pl.BlockSpec(memory_space=m) for m in ins],
        out_specs=tuple(pl.BlockSpec(memory_space=m) for _, m in outs),
        scratch_shapes=scratch,
        cost_estimate=pl.CostEstimate(flops=cost, bytes_accessed=1 << 19, transcendentals=0),
        compiler_params=pltpu.CompilerParams(vmem_limit_bytes=8 << 20),
    )(*args)


def local(velocity, diffusion):
    count_x = lax.axis_size("gx")
    count_y = lax.axis_size("gy")
    tile = (8, LANES)
    n = COMPS * PLANES
    low, high, cells, diff, turned = call(
        edges_kernel,
        (HBM, HBM),
        [
            (shape(*tile), VMEM),
            (shape(*tile), VMEM),
            (shape(COMPS, PLANES, LANES, LANES), VMEM),
            (shape(PLANES, LANES, LANES), VMEM),
            (shape(PLANES, LANES, LANES), VMEM),
        ],
        [pltpu.SemaphoreType.DMA((2,))],
        1 << 17,
        pltpu.with_memory_space_constraint(velocity, HBM),
        pltpu.with_memory_space_constraint(diffusion, HBM),
    )
    from_low = lax.ppermute(high, "gy", [(i, (i + 1) % count_y) for i in range(count_y)])
    from_high = lax.ppermute(low, "gy", [((i + 1) % count_y, i) for i in range(count_y)])
    coef = (shape(PLANES, 3, SEG, *tile), VMEM)
    tree = (shape(PLANES, 3, 3, *tile), VMEM)
    head = (shape(16, LANES), VMEM)
    q_all = (shape(n, SEG, *tile), VMEM)
    q_tree = (shape(n, 3, *tile), VMEM)
    block = VMEM((n, LANES, LANES), f32)
    cx, tx, hx, cy, ty, hy = call(
        matrix_kernel, (VMEM,) * 2, [coef, tree, head] * 2, [], 1 << 21, diff, turned
    )
    sent, qx, qtx = call(
        partial(source_kernel, count_x),
        (VMEM,) * 6,
        [(shape(count_x, ROWS_X, LANES), VMEM), q_all, q_tree],
        [VMEM((LANES, LANES), f32), VMEM((LANES, LANES), f32), VMEM((ROWS_X, LANES), f32)],
        1 << 22,
        cells, from_low, from_high, cx, tx, hx,
    )
    got = lax.all_to_all(sent, "gx", 0, 0)
    sent, qy, qty, own = call(
        partial(middle_kernel, count_x, count_y),
        (VMEM,) * 9,
        [(shape(count_y, ROWS_SENT_Y // 2, 2, LANES), VMEM), q_all, q_tree, head],
        [VMEM((count_x * ROWS_X, LANES), f32), block, block],
        1 << 22,
        got, from_high, cx, tx, qx, qtx, cy, ty, hy,
    )
    got = lax.all_to_all(sent, "gy", 0, 0)
    (result,) = call(
        partial(final_kernel, count_y),
        (VMEM,) * 6,
        [(shape(COMPS, PLANES, LANES, LANES), HBM)],
        [
            VMEM((count_y * ROWS_Y, LANES), f32),
            block,
            block,
            pltpu.SemaphoreType.DMA((n,)),
        ],
        1 << 22,
        got, own, cy, ty, qy, qty,
    )
    return result


def solution(mesh):
    in_specs = (P(None, None, "gx", "gy"), P(None, "gx", "gy"))
    out_specs = P(None, None, "gx", "gy")
    return jax.shard_map(local, mesh=mesh, in_specs=in_specs, out_specs=out_specs, check_vma=False)
```

```python
from functools import partial

import jax
import jax.numpy as jnp
from jax import lax
from jax.experimental import pallas as pl
from jax.experimental.pallas import tpu as pltpu
from jax.sharding import PartitionSpec as P


COURANT = 0.25
HALF = 0.5 * COURANT
SEG = 16
PLANES = 2
COMPS = 3
LANES = 128
ROWS_X = 40
ROWS_Y = 24
ROW_G, ROW_EL, ROW_ER, ROW_DHI, ROW_VLO, ROW_DLO = 0, 2, 4, 6, 8, 14
ROW_JL, ROW_JR, ROW_VHI = 16, 24, 30
TILE_X = 2
SENT_X = [i for i in range(0, 36, TILE_X) if i != 22]
Y_JL, Y_JR, ROWS_SENT_Y = 6, 12, 18
OWN_A, OWN_B, OWN_Q = 0, 2, 4

f32 = jnp.float32
VMEM = pltpu.VMEM
HBM = pltpu.HBM


def sub_iota():
    return lax.broadcasted_iota(jnp.int32, (8, LANES), 0)


def lane_iota():
    return lax.broadcasted_iota(jnp.int32, (8, LANES), 1)


def ahead(x, count):
    return pltpu.roll(x, 8 - count, 0)


def after(x, count):
    return pltpu.roll(x, count, 0)


def strided(ref, lead, t):
    return ref[lead, pl.ds(t, 8, stride=SEG), :]


def factor(cells, first, coef_ref, tree_ref, head_ref, plane):
    row = sub_iota()
    last = row == 7
    faces = [0.5 * (cells[t] + cells[t + 1]) for t in range(SEG - 1)]
    faces.append(0.5 * (cells[SEG - 1] + ahead(cells[0], 1)))
    leak_l = 1.0 + jnp.where(jnp.logical_and(row == 0, first), 0.5 * cells[0], 0.0)
    g = faces[0]
    leak_r = jnp.ones_like(g)
    for t in range(1, SEG):
        f = faces[t]
        inv = 1.0 / (g + f + leak_r)
        a = g * inv
        b = f * inv
        if t == SEG - 1:
            inv = jnp.where(last, 0.0, inv)
            g = jnp.where(last, g, a * f)
            a = jnp.where(last, 0.0, a)
            b = jnp.where(last, 1.0, b)
            leak_l = leak_l + a * leak_r
            leak_r = b * leak_r
        else:
            g = a * f
            leak_l = leak_l + a * leak_r
            leak_r = 1.0 + b * leak_r
        coef_ref[plane, 0, t] = a
        coef_ref[plane, 1, t] = b
        coef_ref[plane, 2, t] = inv
    for level in range(3):
        count = 1 << level
        g_next = ahead(g, count)
        leak = leak_r + ahead(leak_l, count)
        inv = 1.0 / (g + g_next + leak)
        a = g * inv
        b = g_next * inv
        g = a * g_next
        leak_l = leak_l + a * leak
        leak_r = ahead(leak_r, count) + b * leak
        tree_ref[plane, level, 0] = a
        tree_ref[plane, level, 1] = b
        tree_ref[plane, level, 2] = inv
    if head_ref is None:
        return
    for base, value in ((ROW_G, g), (ROW_EL, leak_l), (ROW_ER, leak_r)):
        head_ref[base + plane : base + plane + 1, :] = value[0:1]
    head_ref[ROW_DHI + plane : ROW_DHI + plane + 1, :] = cells[SEG - 1][7:8]
    head_ref[ROW_DLO + plane : ROW_DLO + plane + 1, :] = cells[0][0:1]


def condense(sources, coef_ref, tree_ref, q_ref, qtree_ref, plane, comp):
    k = comp * PLANES + plane
    left = sources[0]
    right = sources[1]
    for t in range(1, SEG):
        q_ref[k, t] = coef_ref[plane, 2, t] * right
        left = left + coef_ref[plane, 0, t] * right
        right = coef_ref[plane, 1, t] * right
        if t < SEG - 1:
            right = right + sources[t + 1]
    for level in range(3):
        count = 1 << level
        j = right + ahead(left, count)
        left = left + tree_ref[plane, level, 0] * j
        right = ahead(right, count) + tree_ref[plane, level, 1] * j
        qtree_ref[k, level] = tree_ref[plane, level, 2] * j
    return left, right


def unfold(low, high, coef_ref, tree_ref, q_ref, qtree_ref, plane, comp, store):
    k = comp * PLANES + plane
    row = sub_iota()

    def mid(level, lo, hi):
        return (
            tree_ref[plane, level, 0] * lo
            + tree_ref[plane, level, 1] * hi
            + qtree_ref[k, level]
        )

    for level in (2, 1, 0):
        count = 1 << level
        between = mid(level, low, high)
        late = (row & count) != 0
        low = jnp.where(late, after(between, count), low)
        high = jnp.where(late, after(high, count), between)
    store(0, low)
    cell = high
    for t in range(SEG - 1, 0, -1):
        cell = (
            coef_ref[plane, 0, t] * low
            + q_ref[k, t]
            + coef_ref[plane, 1, t] * cell
        )
        store(t, cell)


def cyclic(me, half, count):
    return (me + 8 * half + sub_iota()) & (count - 1)


def solve_ring(blocks, me, count):
    halves = []
    for g, leak_l, leak_r, currents in blocks:
        levels = []
        for level in range(3):
            step = 1 << level
            g_next = ahead(g, step)
            leak = leak_r + ahead(leak_l, step)
            inv = 1.0 / (g + g_next + leak)
            a = g * inv
            b = g_next * inv
            g = a * g_next
            leak_l = leak_l + a * leak
            leak_r = ahead(leak_r, step) + b * leak
            levels.append((a, b, inv))
        merged = []
        for left, right in currents:
            terms = []
            for level in range(3):
                step = 1 << level
                a, b, inv = levels[level]
                j = right + ahead(left, step)
                left = left + a * j
                right = ahead(right, step) + b * j
                terms.append(inv * j)
            merged.append((left, right, terms))
        halves.append((g, leak_l, leak_r, levels, merged))
    g, leak_l, leak_r, levels, merged = halves[0]
    g_next, leak_l_next, leak_r_next, _, merged_next = halves[1]
    leak = leak_r + leak_l_next
    inv = 1.0 / (g + g_next + leak)
    a = g * inv
    b = g_next * inv
    total = 1.0 / (leak_l + a * leak + leak_r_next + b * leak)
    ends = []
    for comp in range(COMPS):
        left, right, terms = merged[comp]
        left_next, right_next, _ = merged_next[comp]
        j = right + left_next
        first = (left + a * j + right_next + b * j) * total
        high = (a + b) * first + inv * j
        for level in (2, 1, 0):
            high = levels[level][0] * first + levels[level][1] * high + terms[level]
        ends.append((first, jnp.where(me == count - 1, 0.0, high)))
    return ends


def solve_x(ring_ref, me, count, plane):
    row = sub_iota()

    def take(which, half):
        return ring_ref[pl.ds(8 * half * ROWS_X + which + plane, 8, stride=ROWS_X), :]

    def both(which):
        return take(which, 0), take(which, 1)

    def before(pair, half):
        return jnp.where(row == 0, after(pair[1 - half], 1), after(pair[half], 1))

    def beyond(pair, half):
        return jnp.where(row == 7, ahead(pair[1 - half], 1), ahead(pair[half], 1))

    first_faces = both(ROW_DLO)
    low_cells = [both(ROW_VLO + comp * PLANES) for comp in range(COMPS)]
    high_cells = [both(ROW_VHI + comp * PLANES) for comp in range(COMPS)]
    blocks = []
    own = None
    for half in (0, 1):
        place = cyclic(me, half, count)
        wall = place == count - 1
        g = take(ROW_G, half)
        leak_l = take(ROW_EL, half)
        leak_r = take(ROW_ER, half)
        f = 0.5 * (take(ROW_DHI, half) + jnp.where(wall, 0.0, beyond(first_faces, half)))
        inv = 1.0 / (g + f + leak_r)
        a = g * inv
        b = f * inv
        through = a * f
        leak_l = leak_l + a * leak_r
        leak_l = jnp.where(wall, leak_l + through, leak_l)
        up_lo = jnp.where(place == 0, 0.0, HALF * low_cells[0][half])
        up_hi = jnp.where(wall, 0.0, HALF * high_cells[0][half])
        b_cut = jnp.where(wall, 0.0, b)
        currents = []
        terms = []
        for comp in range(COMPS):
            left = take(ROW_JL + comp * PLANES, half)
            right = take(ROW_JR + comp * PLANES, half)
            left = left + up_lo * before(high_cells[comp], half)
            right = right - up_hi * beyond(low_cells[comp], half)
            terms.append(inv * right)
            currents.append((left + a * right, b_cut * right))
        if half == 0:
            own = (a, b, terms)
        blocks.append((jnp.where(wall, 0.0, through), leak_l, b_cut * leak_r, currents))
    ends = solve_ring(blocks, me, count)
    a, b, terms = own
    return [
        (first, a * first + b * high + terms[comp]) for comp, (first, high) in enumerate(ends)
    ]


def solve_y(ring_ref, own_ref, me, count, plane):
    def take(which, half):
        return ring_ref[pl.ds(8 * half * ROWS_Y + which + plane, 8, stride=ROWS_Y), :]

    def own(which):
        return own_ref[which + plane : which + plane + 1, :]

    blocks = [
        (
            take(ROW_G, half),
            take(ROW_EL, half),
            take(ROW_ER, half),
            [
                (take(Y_JL + comp * PLANES, half), take(Y_JR + comp * PLANES, half))
                for comp in range(COMPS)
            ],
        )
        for half in (0, 1)
    ]
    ends = solve_ring(blocks, me, count)
    return [
        (first, own(OWN_A) * first + own(OWN_B) * high + own(OWN_Q + comp * PLANES))
        for comp, (first, high) in enumerate(ends)
    ]


def edges_kernel(velocity_ref, diffusion_ref, low_ref, high_ref, v_ref, d_ref, turn_ref, sem):
    copies = [
        pltpu.make_async_copy(velocity_ref, v_ref, sem.at[0]),
        pltpu.make_async_copy(diffusion_ref, d_ref, sem.at[1]),
    ]
    for copy in copies:
        copy.start()
    for copy in copies:
        copy.wait()
    for k in range(COMPS * PLANES + PLANES):
        if k < COMPS * PLANES:
            comp, plane = divmod(k, PLANES)
            turned = jnp.transpose(v_ref[comp, plane])
        else:
            turned = jnp.transpose(d_ref[k - 6])
            turn_ref[k - 6] = turned
        low_ref[k : k + 1, :] = turned[0:1]
        high_ref[k : k + 1, :] = turned[LANES - 1 : LANES]


def matrix_kernel(diffusion_ref, turn_ref, low_ref, high_ref, cx_ref, tx_ref, hx_ref, cy_ref, ty_ref,
                  hy_ref, cp_ref, tp_ref, vp_ref, edge_ref, pack_ref):
    first_x = lax.axis_index("gx") == 0
    first_y = lax.axis_index("gy") == 0
    edge_ref[...] = jnp.zeros((2, LANES, LANES), f32)
    for i, base in enumerate((2, 6)):
        for k in range(COMPS * PLANES):
            line = base + k % PLANES
            edge_ref[i, k : k + 1, :] = low_ref[line : line + 1, :]
            edge_ref[i, 8 + k : 9 + k, :] = high_ref[line : line + 1, :]
    vp_ref[...] = jnp.transpose(edge_ref[0])
    pack_ref[0] = jnp.transpose(edge_ref[1])
    for plane in range(PLANES):
        cells = [strided(diffusion_ref, plane, t) for t in range(SEG)]
        factor(cells, first_x, cx_ref, tx_ref, hx_ref, plane)
        cells = [strided(turn_ref, plane, t) for t in range(SEG)]
        factor(cells, first_y, cy_ref, ty_ref, hy_ref, plane)
    cells = [strided(pack_ref, 0, t) for t in range(SEG)]
    factor(cells, first_x, cp_ref, tp_ref, None, 0)
    for ref in (hx_ref, hy_ref):
        ref[ROW_VLO : ROW_VLO + 6, :] = jnp.zeros((6, LANES), f32)


def source_kernel(velocity_ref, coef_ref, tree_ref, head_ref, page_ref, q_ref, qtree_ref):
    row = sub_iota()
    lane = lane_iota()
    page_ref[0:16, :] = head_ref[...]
    page_ref[16:, :] = jnp.zeros((ROWS_X - 16, LANES), f32)
    for plane in range(PLANES):
        cells = [
            [velocity_ref[comp, plane, pl.ds(t, 8, stride=SEG), :] for t in range(SEG)]
            for comp in range(COMPS)
        ]
        for comp in range(COMPS):
            k = comp * PLANES + plane
            own = cells[comp]
            sources = []
            for t in range(SEG):
                if t < SEG - 1:
                    fore = own[t + 1]
                else:
                    fore = jnp.where(row == 7, 0.0, ahead(own[0], 1))
                if t > 0:
                    back = own[t - 1]
                else:
                    back = jnp.where(row == 0, 0.0, after(own[SEG - 1], 1))
                right = jnp.where(lane == LANES - 1, 0.0, pltpu.roll(own[t], LANES - 1, 1))
                left = jnp.where(lane == 0, 0.0, pltpu.roll(own[t], 1, 1))
                sources.append(
                    own[t]
                    - HALF * (cells[0][t] * (fore - back) + cells[1][t] * (right - left))
                )
            left, right = condense(sources, coef_ref, tree_ref, q_ref, qtree_ref, plane, comp)
            page_ref[ROW_JL + k : ROW_JL + k + 1, :] = left[0:1]
            page_ref[ROW_JR + k : ROW_JR + k + 1, :] = right[0:1]
            page_ref[ROW_VLO + k : ROW_VLO + k + 1, :] = own[0][0:1]
            page_ref[ROW_VHI + k : ROW_VHI + k + 1, :] = own[SEG - 1][7:8]


def halo_kernel(count, from_low_ref, from_high_ref, vp_ref, coef_ref, tree_ref, page_ref, out_ref,
                q_ref, qtree_ref, edge_ref, halo_ref):
    me_y = lax.axis_index("gy")
    count_y = lax.axis_size("gy")
    row = sub_iota()
    lane = lane_iota()
    edge_ref[0:8, :] = jnp.where(me_y == 0, 0.0, HALF * from_low_ref[...])
    edge_ref[8:16, :] = jnp.where(me_y == count_y - 1, 0.0, -HALF * from_high_ref[...])
    edge_ref[16:, :] = jnp.zeros((LANES - 16, LANES), f32)
    halo_ref[...] = jnp.transpose(edge_ref[...])
    sources = [
        vp_ref[pl.ds(t, 8, stride=SEG), :] * halo_ref[pl.ds(t, 8, stride=SEG), :]
        for t in range(SEG)
    ]
    ends = condense(sources, coef_ref, tree_ref, q_ref, qtree_ref, 0, 0)
    page = [page_ref[8 * i : 8 * i + 8, :] for i in range(ROWS_X // 8)]
    for base, value in zip((ROW_JL, ROW_JR), ends):
        value = jnp.broadcast_to(value[0:1], (8, LANES))
        low = jnp.sum(jnp.where(lane == row, value, 0.0), axis=1, keepdims=True)
        high = jnp.sum(jnp.where(lane == row + 8, value, 0.0), axis=1, keepdims=True)
        extra = jnp.where(lane == 0, low, jnp.where(lane == LANES - 1, high, 0.0))
        page[base // 8] = page[base // 8] + extra
    for i, rows in enumerate(page):
        edge_ref[8 * i : 8 * i + 8, :] = rows
    for j, start in enumerate(SENT_X):
        rows = edge_ref[start : start + TILE_X, :]
        for i in range(count):
            out_ref[i, j] = rows


def middle_kernel(count_x, count_y, got_ref, from_high_ref, cx_ref, tx_ref, qx_ref, qtx_ref, cy_ref,
                  ty_ref, hy_ref, cp_ref, tp_ref, qp_ref, qtp_ref, out_ref, q_ref, qtree_ref, own_ref,
                  ring_ref, plane_ref, turn_ref, pack_ref, extra_ref):
    me = lax.axis_index("gx")

    def store_pack(t, value):
        pack_ref[pl.ds(t, 8, stride=SEG), :] = value

    nothing = jnp.zeros((8, LANES), f32)
    unfold(nothing, nothing, cp_ref, tp_ref, qp_ref, qtp_ref, 0, 0, store_pack)
    extra_ref[...] = jnp.transpose(pack_ref[...])
    wall = lax.axis_index("gy") == count_y - 1
    for i in range(count_x):
        slot = (i - me + count_x) & (count_x - 1)
        base = slot * ROWS_X
        for j, start in enumerate(SENT_X):
            ring_ref[pl.ds(base + start, TILE_X), :] = got_ref[i, j]
    own_ref[10:16, :] = jnp.zeros((6, LANES), f32)
    values = {}
    for plane in range(PLANES):

        def head(which):
            return hy_ref[which + plane : which + plane + 1, :]

        g = head(ROW_G)
        leak_r = head(ROW_ER)
        beyond = from_high_ref[6 + plane : 7 + plane, :]
        f = 0.5 * (head(ROW_DHI) + jnp.where(wall, 0.0, beyond))
        inv = 1.0 / (g + f + leak_r)
        a = g * inv
        b = f * inv
        through = a * f
        b_cut = jnp.where(wall, 0.0, b)
        own_ref[OWN_A + plane : OWN_A + plane + 1, :] = a
        own_ref[OWN_B + plane : OWN_B + plane + 1, :] = b
        values[ROW_G + plane] = jnp.where(wall, 0.0, through)
        leak_l = head(ROW_EL) + a * leak_r
        values[ROW_EL + plane] = jnp.where(wall, leak_l + through, leak_l)
        values[ROW_ER + plane] = b_cut * leak_r
        ends = solve_x(ring_ref, me, count_x, plane)
        for comp in range(COMPS):
            k = comp * PLANES + plane
            low, high = ends[comp]

            def store(t, value):
                plane_ref[k, pl.ds(t, 8, stride=SEG), :] = value

            unfold(low, high, cx_ref, tx_ref, qx_ref, qtx_ref, plane, comp, store)
            turned = jnp.transpose(plane_ref[k])
            turn_ref[k] = turned
            turn_ref[k, 0:1, :] = turned[0:1] + extra_ref[k : k + 1, :]
            turn_ref[k, LANES - 1 :, :] = turned[LANES - 1 :] + extra_ref[8 + k : 9 + k, :]
            sources = [strided(turn_ref, k, t) for t in range(SEG)]
            left, right = condense(sources, cy_ref, ty_ref, q_ref, qtree_ref, plane, comp)
            right = right[0:1]
            own_ref[OWN_Q + k : OWN_Q + k + 1, :] = inv * right
            values[Y_JL + k] = left[0:1] + a * right
            values[Y_JR + k] = b_cut * right
    for pair in range(ROWS_SENT_Y // 2):
        rows = jnp.concatenate([values[2 * pair], values[2 * pair + 1]], 0)
        for i in range(count_y):
            out_ref[i, pair] = rows


def final_kernel(count, got_ref, own_ref, coef_ref, tree_ref, q_ref, qtree_ref, out_ref, ring_ref,
                 plane_ref, turn_ref, sem):
    me = lax.axis_index("gy")
    for i in range(count):
        slot = (i - me + count) & (count - 1)
        base = slot * ROWS_Y
        for pair in range(ROWS_SENT_Y // 2):
            ring_ref[pl.ds(base + 2 * pair, 2), :] = got_ref[i, pair]
    copies = []
    for plane in range(PLANES):
        ends = solve_y(ring_ref, own_ref, me, count, plane)
        for comp in range(COMPS):
            k = comp * PLANES + plane
            low, high = ends[comp]

            def store(t, value):
                plane_ref[k, pl.ds(t, 8, stride=SEG), :] = value

            unfold(low, high, coef_ref, tree_ref, q_ref, qtree_ref, plane, comp, store)
            turn_ref[k] = jnp.transpose(plane_ref[k])
            copy = pltpu.make_async_copy(turn_ref.at[k], out_ref.at[comp, plane], sem.at[k])
            copy.start()
            copies.append(copy)
    for copy in copies:
        copy.wait()


def shape(*dims):
    return jax.ShapeDtypeStruct(dims, f32)


def call(kernel, ins, outs, scratch, cost, *args):
    return pl.pallas_call(
        kernel,
        out_shape=tuple(o for o, _ in outs),
        in_specs=[pl.BlockSpec(memory_space=m) for m in ins],
        out_specs=tuple(pl.BlockSpec(memory_space=m) for _, m in outs),
        scratch_shapes=scratch,
        cost_estimate=pl.CostEstimate(flops=cost, bytes_accessed=1 << 19, transcendentals=0),
        compiler_params=pltpu.CompilerParams(vmem_limit_bytes=8 << 20),
    )(*args)


def local(velocity, diffusion):
    count_x = lax.axis_size("gx")
    count_y = lax.axis_size("gy")
    tile = (8, LANES)
    n = COMPS * PLANES
    low, high, cells, diff, turned = call(
        edges_kernel,
        (HBM, HBM),
        [
            (shape(*tile), VMEM),
            (shape(*tile), VMEM),
            (shape(COMPS, PLANES, LANES, LANES), VMEM),
            (shape(PLANES, LANES, LANES), VMEM),
            (shape(PLANES, LANES, LANES), VMEM),
        ],
        [pltpu.SemaphoreType.DMA((2,))],
        1 << 17,
        pltpu.with_memory_space_constraint(velocity, HBM),
        pltpu.with_memory_space_constraint(diffusion, HBM),
    )
    from_low = lax.ppermute(high, "gy", [(i, (i + 1) % count_y) for i in range(count_y)])
    from_high = lax.ppermute(low, "gy", [((i + 1) % count_y, i) for i in range(count_y)])
    coef = (shape(PLANES, 3, SEG, *tile), VMEM)
    tree = (shape(PLANES, 3, 3, *tile), VMEM)
    head = (shape(16, LANES), VMEM)
    q_all = (shape(n, SEG, *tile), VMEM)
    q_tree = (shape(n, 3, *tile), VMEM)
    block = VMEM((n, LANES, LANES), f32)
    square = VMEM((LANES, LANES), f32)
    pair = VMEM((PLANES, LANES, LANES), f32)
    coef_pack = (shape(1, 3, SEG, *tile), VMEM)
    tree_pack = (shape(1, 3, 3, *tile), VMEM)
    cx, tx, hx, cy, ty, hy, cp, tp, vp = call(
        matrix_kernel,
        (VMEM,) * 4,
        [coef, tree, head] * 2 + [coef_pack, tree_pack, (shape(LANES, LANES), VMEM)],
        [pair, pair],
        1 << 21,
        diff, turned, low, high,
    )
    page, qx, qtx = call(
        source_kernel,
        (VMEM,) * 4,
        [(shape(ROWS_X, LANES), VMEM), q_all, q_tree],
        [],
        1 << 22,
        cells, cx, tx, hx,
    )
    sent, qp, qtp = call(
        partial(halo_kernel, count_x),
        (VMEM,) * 6,
        [
            (shape(count_x, len(SENT_X), TILE_X, LANES), VMEM),
            (shape(1, SEG, *tile), VMEM),
            (shape(1, 3, *tile), VMEM),
        ],
        [square, square],
        1 << 18,
        from_low, from_high, vp, cp, tp, page,
    )
    got = lax.all_to_all(sent, "gx", 0, 0)
    sent, qy, qty, own = call(
        partial(middle_kernel, count_x, count_y),
        (VMEM,) * 13,
        [(shape(count_y, ROWS_SENT_Y // 2, 2, LANES), VMEM), q_all, q_tree, head],
        [VMEM((count_x * ROWS_X, LANES), f32), block, block, square, square],
        1 << 22,
        got, from_high, cx, tx, qx, qtx, cy, ty, hy, cp, tp, qp, qtp,
    )
    got = lax.all_to_all(sent, "gy", 0, 0)
    (result,) = call(
        partial(final_kernel, count_y),
        (VMEM,) * 6,
        [(shape(COMPS, PLANES, LANES, LANES), HBM)],
        [
            VMEM((count_y * ROWS_Y, LANES), f32),
            block,
            block,
            pltpu.SemaphoreType.DMA((n,)),
        ],
        1 << 22,
        got, own, cy, ty, qy, qty,
    )
    return result


def solution(mesh):
    in_specs = (P(None, None, "gx", "gy"), P(None, "gx", "gy"))
    out_specs = P(None, None, "gx", "gy")
    return jax.shard_map(local, mesh=mesh, in_specs=in_specs, out_specs=out_specs, check_vma=False)
```

```python
from functools import partial

import jax
import jax.numpy as jnp
from jax import lax
from jax.experimental import pallas as pl
from jax.experimental.pallas import tpu as pltpu
from jax.sharding import PartitionSpec as P


COURANT = 0.25
HALF = 0.5 * COURANT
SEG = 16
PLANES = 2
COMPS = 3
LANES = 128
ROWS_X = 40
ROWS_Y = 24
ROW_G, ROW_EL, ROW_ER, ROW_DHI, ROW_VLO, ROW_DLO = 0, 2, 4, 6, 8, 14
ROW_JL, ROW_JR, ROW_VHI = 16, 24, 30
TILE_X = 2
SENT_X = [i for i in range(0, 36, TILE_X) if i != 22]
Y_JL, Y_JR, ROWS_SENT_Y = 6, 12, 18
OWN_A, OWN_B, OWN_Q = 0, 2, 4

f32 = jnp.float32
VMEM = pltpu.VMEM
HBM = pltpu.HBM


def sub_iota():
    return lax.broadcasted_iota(jnp.int32, (8, LANES), 0)


def lane_iota():
    return lax.broadcasted_iota(jnp.int32, (8, LANES), 1)


def ahead(x, count):
    return pltpu.roll(x, 8 - count, 0)


def after(x, count):
    return pltpu.roll(x, count, 0)


def strided(ref, lead, t):
    return ref[lead, pl.ds(t, 8, stride=SEG), :]


def factor(cells, first, coef_ref, tree_ref, head_ref, plane):
    row = sub_iota()
    last = row == 7
    faces = [0.5 * (cells[t] + cells[t + 1]) for t in range(SEG - 1)]
    faces.append(0.5 * (cells[SEG - 1] + ahead(cells[0], 1)))
    leak_l = 1.0 + jnp.where(jnp.logical_and(row == 0, first), 0.5 * cells[0], 0.0)
    g = faces[0]
    leak_r = jnp.ones_like(g)
    for t in range(1, SEG):
        f = faces[t]
        inv = 1.0 / (g + f + leak_r)
        a = g * inv
        b = f * inv
        if t == SEG - 1:
            inv = jnp.where(last, 0.0, inv)
            g = jnp.where(last, g, a * f)
            a = jnp.where(last, 0.0, a)
            b = jnp.where(last, 1.0, b)
            leak_l = leak_l + a * leak_r
            leak_r = b * leak_r
        else:
            g = a * f
            leak_l = leak_l + a * leak_r
            leak_r = 1.0 + b * leak_r
        coef_ref[plane, 0, t] = a
        coef_ref[plane, 1, t] = b
        coef_ref[plane, 2, t] = inv
    for level in range(3):
        count = 1 << level
        g_next = ahead(g, count)
        leak = leak_r + ahead(leak_l, count)
        inv = 1.0 / (g + g_next + leak)
        a = g * inv
        b = g_next * inv
        g = a * g_next
        leak_l = leak_l + a * leak
        leak_r = ahead(leak_r, count) + b * leak
        tree_ref[plane, level, 0] = a
        tree_ref[plane, level, 1] = b
        tree_ref[plane, level, 2] = inv
    if head_ref is None:
        return
    for base, value in ((ROW_G, g), (ROW_EL, leak_l), (ROW_ER, leak_r)):
        head_ref[base + plane : base + plane + 1, :] = value[0:1]
    head_ref[ROW_DHI + plane : ROW_DHI + plane + 1, :] = cells[SEG - 1][7:8]
    head_ref[ROW_DLO + plane : ROW_DLO + plane + 1, :] = cells[0][0:1]


def condense(sources, coef_ref, tree_ref, q_ref, qtree_ref, plane, comp):
    k = comp * PLANES + plane
    left = sources[0]
    right = sources[1]
    for t in range(1, SEG):
        q_ref[k, t] = coef_ref[plane, 2, t] * right
        left = left + coef_ref[plane, 0, t] * right
        right = coef_ref[plane, 1, t] * right
        if t < SEG - 1:
            right = right + sources[t + 1]
    for level in range(3):
        count = 1 << level
        j = right + ahead(left, count)
        left = left + tree_ref[plane, level, 0] * j
        right = ahead(right, count) + tree_ref[plane, level, 1] * j
        qtree_ref[k, level] = tree_ref[plane, level, 2] * j
    return left, right


def unfold(low, high, coef_ref, tree_ref, q_ref, qtree_ref, plane, comp, store):
    k = comp * PLANES + plane
    row = sub_iota()

    def mid(level, lo, hi):
        return (
            tree_ref[plane, level, 0] * lo
            + tree_ref[plane, level, 1] * hi
            + qtree_ref[k, level]
        )

    for level in (2, 1, 0):
        count = 1 << level
        between = mid(level, low, high)
        late = (row & count) != 0
        low = jnp.where(late, after(between, count), low)
        high = jnp.where(late, after(high, count), between)
    store(0, low)
    cell = high
    for t in range(SEG - 1, 0, -1):
        cell = (
            coef_ref[plane, 0, t] * low
            + q_ref[k, t]
            + coef_ref[plane, 1, t] * cell
        )
        store(t, cell)


def cyclic(me, half, count):
    return (me + 8 * half + sub_iota()) & (count - 1)


def solve_ring(blocks, me, count):
    halves = []
    for g, leak_l, leak_r, currents in blocks:
        levels = []
        for level in range(3):
            step = 1 << level
            g_next = ahead(g, step)
            leak = leak_r + ahead(leak_l, step)
            inv = 1.0 / (g + g_next + leak)
            a = g * inv
            b = g_next * inv
            g = a * g_next
            leak_l = leak_l + a * leak
            leak_r = ahead(leak_r, step) + b * leak
            levels.append((a, b, inv))
        merged = []
        for left, right in currents:
            terms = []
            for level in range(3):
                step = 1 << level
                a, b, inv = levels[level]
                j = right + ahead(left, step)
                left = left + a * j
                right = ahead(right, step) + b * j
                terms.append(inv * j)
            merged.append((left, right, terms))
        halves.append((g, leak_l, leak_r, levels, merged))
    g, leak_l, leak_r, levels, merged = halves[0]
    g_next, leak_l_next, leak_r_next, _, merged_next = halves[1]
    leak = leak_r + leak_l_next
    inv = 1.0 / (g + g_next + leak)
    a = g * inv
    b = g_next * inv
    total = 1.0 / (leak_l + a * leak + leak_r_next + b * leak)
    ends = []
    for comp in range(COMPS):
        left, right, terms = merged[comp]
        left_next, right_next, _ = merged_next[comp]
        j = right + left_next
        first = (left + a * j + right_next + b * j) * total
        high = (a + b) * first + inv * j
        for level in (2, 1, 0):
            high = levels[level][0] * first + levels[level][1] * high + terms[level]
        ends.append((first, jnp.where(me == count - 1, 0.0, high)))
    return ends


def solve_x(ring_ref, me, count, plane):
    row = sub_iota()

    def take(which, half):
        return ring_ref[pl.ds(8 * half * ROWS_X + which + plane, 8, stride=ROWS_X), :]

    def both(which):
        return take(which, 0), take(which, 1)

    def before(pair, half):
        return jnp.where(row == 0, after(pair[1 - half], 1), after(pair[half], 1))

    def beyond(pair, half):
        return jnp.where(row == 7, ahead(pair[1 - half], 1), ahead(pair[half], 1))

    first_faces = both(ROW_DLO)
    low_cells = [both(ROW_VLO + comp * PLANES) for comp in range(COMPS)]
    high_cells = [both(ROW_VHI + comp * PLANES) for comp in range(COMPS)]
    blocks = []
    own = None
    for half in (0, 1):
        place = cyclic(me, half, count)
        wall = place == count - 1
        g = take(ROW_G, half)
        leak_l = take(ROW_EL, half)
        leak_r = take(ROW_ER, half)
        f = 0.5 * (take(ROW_DHI, half) + jnp.where(wall, 0.0, beyond(first_faces, half)))
        inv = 1.0 / (g + f + leak_r)
        a = g * inv
        b = f * inv
        through = a * f
        leak_l = leak_l + a * leak_r
        leak_l = jnp.where(wall, leak_l + through, leak_l)
        up_lo = jnp.where(place == 0, 0.0, HALF * low_cells[0][half])
        up_hi = jnp.where(wall, 0.0, HALF * high_cells[0][half])
        b_cut = jnp.where(wall, 0.0, b)
        currents = []
        terms = []
        for comp in range(COMPS):
            left = take(ROW_JL + comp * PLANES, half)
            right = take(ROW_JR + comp * PLANES, half)
            left = left + up_lo * before(high_cells[comp], half)
            right = right - up_hi * beyond(low_cells[comp], half)
            terms.append(inv * right)
            currents.append((left + a * right, b_cut * right))
        if half == 0:
            own = (a, b, terms)
        blocks.append((jnp.where(wall, 0.0, through), leak_l, b_cut * leak_r, currents))
    ends = solve_ring(blocks, me, count)
    a, b, terms = own
    return [
        (first, a * first + b * high + terms[comp]) for comp, (first, high) in enumerate(ends)
    ]


def solve_y(ring_ref, own_ref, me, count, plane):
    def take(which, half):
        return ring_ref[pl.ds(8 * half * ROWS_Y + which + plane, 8, stride=ROWS_Y), :]

    def own(which):
        return own_ref[which + plane : which + plane + 1, :]

    blocks = [
        (
            take(ROW_G, half),
            take(ROW_EL, half),
            take(ROW_ER, half),
            [
                (take(Y_JL + comp * PLANES, half), take(Y_JR + comp * PLANES, half))
                for comp in range(COMPS)
            ],
        )
        for half in (0, 1)
    ]
    ends = solve_ring(blocks, me, count)
    return [
        (first, own(OWN_A) * first + own(OWN_B) * high + own(OWN_Q + comp * PLANES))
        for comp, (first, high) in enumerate(ends)
    ]


def by_parity(even, odd):
    return jnp.where(lax.axis_index("gy") % 2 == 0, even, odd)


def edges_kernel(velocity_ref, diffusion_ref, low_ref, high_ref, near_ref, far_ref, v_ref, d_ref,
                 turn_ref, sem):
    copies = [
        pltpu.make_async_copy(velocity_ref, v_ref, sem.at[0]),
        pltpu.make_async_copy(diffusion_ref, d_ref, sem.at[1]),
    ]
    for copy in copies:
        copy.start()
    for copy in copies:
        copy.wait()
    for k in range(COMPS * PLANES + PLANES):
        if k < COMPS * PLANES:
            comp, plane = divmod(k, PLANES)
            turned = jnp.transpose(v_ref[comp, plane])
        else:
            turned = jnp.transpose(d_ref[k - 6])
            turn_ref[k - 6] = turned
        low = turned[0:1]
        high = turned[LANES - 1 : LANES]
        low_ref[k : k + 1, :] = low
        high_ref[k : k + 1, :] = high
        near_ref[k : k + 1, :] = by_parity(high, low)
        far_ref[k : k + 1, :] = by_parity(low, high)


def matrix_kernel(diffusion_ref, turn_ref, low_ref, high_ref, cx_ref, tx_ref, hx_ref, cy_ref, ty_ref,
                  hy_ref, cp_ref, tp_ref, vp_ref, edge_ref, pack_ref):
    first_x = lax.axis_index("gx") == 0
    first_y = lax.axis_index("gy") == 0
    edge_ref[...] = jnp.zeros((2, LANES, LANES), f32)
    for i, base in enumerate((2, 6)):
        for k in range(COMPS * PLANES):
            line = base + k % PLANES
            edge_ref[i, k : k + 1, :] = low_ref[line : line + 1, :]
            edge_ref[i, 8 + k : 9 + k, :] = high_ref[line : line + 1, :]
    vp_ref[...] = jnp.transpose(edge_ref[0])
    pack_ref[0] = jnp.transpose(edge_ref[1])
    for plane in range(PLANES):
        cells = [strided(diffusion_ref, plane, t) for t in range(SEG)]
        factor(cells, first_x, cx_ref, tx_ref, hx_ref, plane)
        cells = [strided(turn_ref, plane, t) for t in range(SEG)]
        factor(cells, first_y, cy_ref, ty_ref, hy_ref, plane)
    cells = [strided(pack_ref, 0, t) for t in range(SEG)]
    factor(cells, first_x, cp_ref, tp_ref, None, 0)
    for ref in (hx_ref, hy_ref):
        ref[ROW_VLO : ROW_VLO + 6, :] = jnp.zeros((6, LANES), f32)


def source_kernel(velocity_ref, coef_ref, tree_ref, head_ref, page_ref, q_ref, qtree_ref):
    row = sub_iota()
    lane = lane_iota()
    page_ref[0:16, :] = head_ref[...]
    page_ref[16:, :] = jnp.zeros((ROWS_X - 16, LANES), f32)
    for plane in range(PLANES):
        cells = [
            [velocity_ref[comp, plane, pl.ds(t, 8, stride=SEG), :] for t in range(SEG)]
            for comp in range(COMPS)
        ]
        for comp in range(COMPS):
            k = comp * PLANES + plane
            own = cells[comp]
            sources = []
            for t in range(SEG):
                if t < SEG - 1:
                    fore = own[t + 1]
                else:
                    fore = jnp.where(row == 7, 0.0, ahead(own[0], 1))
                if t > 0:
                    back = own[t - 1]
                else:
                    back = jnp.where(row == 0, 0.0, after(own[SEG - 1], 1))
                right = jnp.where(lane == LANES - 1, 0.0, pltpu.roll(own[t], LANES - 1, 1))
                left = jnp.where(lane == 0, 0.0, pltpu.roll(own[t], 1, 1))
                sources.append(
                    own[t]
                    - HALF * (cells[0][t] * (fore - back) + cells[1][t] * (right - left))
                )
            left, right = condense(sources, coef_ref, tree_ref, q_ref, qtree_ref, plane, comp)
            page_ref[ROW_JL + k : ROW_JL + k + 1, :] = left[0:1]
            page_ref[ROW_JR + k : ROW_JR + k + 1, :] = right[0:1]
            page_ref[ROW_VLO + k : ROW_VLO + k + 1, :] = own[0][0:1]
            page_ref[ROW_VHI + k : ROW_VHI + k + 1, :] = own[SEG - 1][7:8]


def halo_kernel(count, from_near_ref, from_far_ref, vp_ref, coef_ref, tree_ref, page_ref, out_ref,
                q_ref, qtree_ref, edge_ref, halo_ref):
    me_y = lax.axis_index("gy")
    count_y = lax.axis_size("gy")
    row = sub_iota()
    lane = lane_iota()
    near = from_near_ref[...]
    far = from_far_ref[...]
    edge_ref[0:8, :] = jnp.where(me_y == 0, 0.0, HALF * by_parity(far, near))
    edge_ref[8:16, :] = jnp.where(me_y == count_y - 1, 0.0, -HALF * by_parity(near, far))
    edge_ref[16:, :] = jnp.zeros((LANES - 16, LANES), f32)
    halo_ref[...] = jnp.transpose(edge_ref[...])
    sources = [
        vp_ref[pl.ds(t, 8, stride=SEG), :] * halo_ref[pl.ds(t, 8, stride=SEG), :]
        for t in range(SEG)
    ]
    ends = condense(sources, coef_ref, tree_ref, q_ref, qtree_ref, 0, 0)
    page = [page_ref[8 * i : 8 * i + 8, :] for i in range(ROWS_X // 8)]
    for base, value in zip((ROW_JL, ROW_JR), ends):
        value = jnp.broadcast_to(value[0:1], (8, LANES))
        low = jnp.sum(jnp.where(lane == row, value, 0.0), axis=1, keepdims=True)
        high = jnp.sum(jnp.where(lane == row + 8, value, 0.0), axis=1, keepdims=True)
        extra = jnp.where(lane == 0, low, jnp.where(lane == LANES - 1, high, 0.0))
        page[base // 8] = page[base // 8] + extra
    for i, rows in enumerate(page):
        edge_ref[8 * i : 8 * i + 8, :] = rows
    for j, start in enumerate(SENT_X):
        rows = edge_ref[start : start + TILE_X, :]
        for i in range(count):
            out_ref[i, j] = rows


def middle_kernel(count_x, count_y, got_ref, from_near_ref, from_far_ref, cx_ref, tx_ref, qx_ref, qtx_ref, cy_ref,
                  ty_ref, hy_ref, cp_ref, tp_ref, qp_ref, qtp_ref, out_ref, q_ref, qtree_ref, own_ref,
                  ring_ref, plane_ref, turn_ref, pack_ref, extra_ref):
    me = lax.axis_index("gx")

    def store_pack(t, value):
        pack_ref[pl.ds(t, 8, stride=SEG), :] = value

    nothing = jnp.zeros((8, LANES), f32)
    unfold(nothing, nothing, cp_ref, tp_ref, qp_ref, qtp_ref, 0, 0, store_pack)
    extra_ref[...] = jnp.transpose(pack_ref[...])
    wall = lax.axis_index("gy") == count_y - 1
    for i in range(count_x):
        slot = (i - me + count_x) & (count_x - 1)
        base = slot * ROWS_X
        for j, start in enumerate(SENT_X):
            ring_ref[pl.ds(base + start, TILE_X), :] = got_ref[i, j]
    own_ref[10:16, :] = jnp.zeros((6, LANES), f32)
    values = {}
    for plane in range(PLANES):

        def head(which):
            return hy_ref[which + plane : which + plane + 1, :]

        g = head(ROW_G)
        leak_r = head(ROW_ER)
        line = slice(6 + plane, 7 + plane)
        beyond = by_parity(from_near_ref[line, :], from_far_ref[line, :])
        f = 0.5 * (head(ROW_DHI) + jnp.where(wall, 0.0, beyond))
        inv = 1.0 / (g + f + leak_r)
        a = g * inv
        b = f * inv
        through = a * f
        b_cut = jnp.where(wall, 0.0, b)
        own_ref[OWN_A + plane : OWN_A + plane + 1, :] = a
        own_ref[OWN_B + plane : OWN_B + plane + 1, :] = b
        values[ROW_G + plane] = jnp.where(wall, 0.0, through)
        leak_l = head(ROW_EL) + a * leak_r
        values[ROW_EL + plane] = jnp.where(wall, leak_l + through, leak_l)
        values[ROW_ER + plane] = b_cut * leak_r
        ends = solve_x(ring_ref, me, count_x, plane)
        for comp in range(COMPS):
            k = comp * PLANES + plane
            low, high = ends[comp]

            def store(t, value):
                plane_ref[k, pl.ds(t, 8, stride=SEG), :] = value

            unfold(low, high, cx_ref, tx_ref, qx_ref, qtx_ref, plane, comp, store)
            turned = jnp.transpose(plane_ref[k])
            turn_ref[k] = turned
            turn_ref[k, 0:1, :] = turned[0:1] + extra_ref[k : k + 1, :]
            turn_ref[k, LANES - 1 :, :] = turned[LANES - 1 :] + extra_ref[8 + k : 9 + k, :]
            sources = [strided(turn_ref, k, t) for t in range(SEG)]
            left, right = condense(sources, cy_ref, ty_ref, q_ref, qtree_ref, plane, comp)
            right = right[0:1]
            own_ref[OWN_Q + k : OWN_Q + k + 1, :] = inv * right
            values[Y_JL + k] = left[0:1] + a * right
            values[Y_JR + k] = b_cut * right
    for pair in range(ROWS_SENT_Y // 2):
        rows = jnp.concatenate([values[2 * pair], values[2 * pair + 1]], 0)
        for i in range(count_y):
            out_ref[i, pair] = rows


def final_kernel(count, got_ref, own_ref, coef_ref, tree_ref, q_ref, qtree_ref, out_ref, ring_ref,
                 plane_ref, turn_ref, sem):
    me = lax.axis_index("gy")
    for i in range(count):
        slot = (i - me + count) & (count - 1)
        base = slot * ROWS_Y
        for pair in range(ROWS_SENT_Y // 2):
            ring_ref[pl.ds(base + 2 * pair, 2), :] = got_ref[i, pair]
    copies = []
    for plane in range(PLANES):
        ends = solve_y(ring_ref, own_ref, me, count, plane)
        for comp in range(COMPS):
            k = comp * PLANES + plane
            low, high = ends[comp]

            def store(t, value):
                plane_ref[k, pl.ds(t, 8, stride=SEG), :] = value

            unfold(low, high, coef_ref, tree_ref, q_ref, qtree_ref, plane, comp, store)
            turn_ref[k] = jnp.transpose(plane_ref[k])
            copy = pltpu.make_async_copy(turn_ref.at[k], out_ref.at[comp, plane], sem.at[k])
            copy.start()
            copies.append(copy)
    for copy in copies:
        copy.wait()


def shape(*dims):
    return jax.ShapeDtypeStruct(dims, f32)


def call(kernel, ins, outs, scratch, cost, *args):
    return pl.pallas_call(
        kernel,
        out_shape=tuple(o for o, _ in outs),
        in_specs=[pl.BlockSpec(memory_space=m) for m in ins],
        out_specs=tuple(pl.BlockSpec(memory_space=m) for _, m in outs),
        scratch_shapes=scratch,
        cost_estimate=pl.CostEstimate(flops=cost, bytes_accessed=1 << 19, transcendentals=0),
        compiler_params=pltpu.CompilerParams(vmem_limit_bytes=8 << 20),
    )(*args)


def local(velocity, diffusion):
    count_x = lax.axis_size("gx")
    count_y = lax.axis_size("gy")
    tile = (8, LANES)
    n = COMPS * PLANES
    low, high, near, far, cells, diff, turned = call(
        edges_kernel,
        (HBM, HBM),
        [
            (shape(*tile), VMEM),
            (shape(*tile), VMEM),
            (shape(*tile), VMEM),
            (shape(*tile), VMEM),
            (shape(COMPS, PLANES, LANES, LANES), VMEM),
            (shape(PLANES, LANES, LANES), VMEM),
            (shape(PLANES, LANES, LANES), VMEM),
        ],
        [pltpu.SemaphoreType.DMA((2,))],
        1 << 17,
        pltpu.with_memory_space_constraint(velocity, HBM),
        pltpu.with_memory_space_constraint(diffusion, HBM),
    )
    ring = range(count_y)
    from_far = lax.ppermute(far, "gy", [(i, (i - 1 + 2 * (i % 2)) % count_y) for i in ring])
    from_near = lax.ppermute(near, "gy", [(i, i ^ 1) for i in ring])
    coef = (shape(PLANES, 3, SEG, *tile), VMEM)
    tree = (shape(PLANES, 3, 3, *tile), VMEM)
    head = (shape(16, LANES), VMEM)
    q_all = (shape(n, SEG, *tile), VMEM)
    q_tree = (shape(n, 3, *tile), VMEM)
    block = VMEM((n, LANES, LANES), f32)
    square = VMEM((LANES, LANES), f32)
    pair = VMEM((PLANES, LANES, LANES), f32)
    coef_pack = (shape(1, 3, SEG, *tile), VMEM)
    tree_pack = (shape(1, 3, 3, *tile), VMEM)
    cx, tx, hx, cy, ty, hy, cp, tp, vp = call(
        matrix_kernel,
        (VMEM,) * 4,
        [coef, tree, head] * 2 + [coef_pack, tree_pack, (shape(LANES, LANES), VMEM)],
        [pair, pair],
        1 << 21,
        diff, turned, low, high,
    )
    page, qx, qtx = call(
        source_kernel,
        (VMEM,) * 4,
        [(shape(ROWS_X, LANES), VMEM), q_all, q_tree],
        [],
        1 << 22,
        cells, cx, tx, hx,
    )
    sent, qp, qtp = call(
        partial(halo_kernel, count_x),
        (VMEM,) * 6,
        [
            (shape(count_x, len(SENT_X), TILE_X, LANES), VMEM),
            (shape(1, SEG, *tile), VMEM),
            (shape(1, 3, *tile), VMEM),
        ],
        [square, square],
        1 << 18,
        from_near, from_far, vp, cp, tp, page,
    )
    got = lax.all_to_all(sent, "gx", 0, 0)
    sent, qy, qty, own = call(
        partial(middle_kernel, count_x, count_y),
        (VMEM,) * 14,
        [(shape(count_y, ROWS_SENT_Y // 2, 2, LANES), VMEM), q_all, q_tree, head],
        [VMEM((count_x * ROWS_X, LANES), f32), block, block, square, square],
        1 << 22,
        got, from_near, from_far, cx, tx, qx, qtx, cy, ty, hy, cp, tp, qp, qtp,
    )
    got = lax.all_to_all(sent, "gy", 0, 0)
    (result,) = call(
        partial(final_kernel, count_y),
        (VMEM,) * 6,
        [(shape(COMPS, PLANES, LANES, LANES), HBM)],
        [
            VMEM((count_y * ROWS_Y, LANES), f32),
            block,
            block,
            pltpu.SemaphoreType.DMA((n,)),
        ],
        1 << 22,
        got, own, cy, ty, qy, qty,
    )
    return result


def solution(mesh):
    in_specs = (P(None, None, "gx", "gy"), P(None, "gx", "gy"))
    out_specs = P(None, None, "gx", "gy")
    return jax.shard_map(local, mesh=mesh, in_specs=in_specs, out_specs=out_specs, check_vma=False)
```

```python
from functools import partial

import jax
import jax.numpy as jnp
from jax import lax
from jax.experimental import pallas as pl
from jax.experimental.pallas import tpu as pltpu
from jax.sharding import PartitionSpec as P


COURANT = 0.25
HALF = 0.5 * COURANT
SEG = 16
PLANES = 2
COMPS = 3
LANES = 128
PITCH = 18
ROWS_X = 34
ROWS_Y = 18
ROW_G, ROW_EL, ROW_ER, ROW_DHI, ROW_VLO, ROW_DLO = 0, 2, 4, 6, 8, 14
ROW_JL, ROW_JR, ROW_VHI = 16, 22, 28
Y_JL, Y_JR = 6, 12
OWN_A, OWN_B, OWN_Q = 0, 2, 4

f32 = jnp.float32
VMEM = pltpu.VMEM
HBM = pltpu.HBM


def sub_iota():
    return lax.broadcasted_iota(jnp.int32, (8, LANES), 0)


def lane_iota():
    return lax.broadcasted_iota(jnp.int32, (8, LANES), 1)


def ahead(x, count):
    return pltpu.roll(x, 8 - count, 0)


def after(x, count):
    return pltpu.roll(x, count, 0)


def strided(ref, lead, t):
    return ref[lead, pl.ds(t, 8, stride=SEG), :]


def segment(t):
    return pl.ds(t, 8, stride=PITCH)


def natural(ref, lead):
    starts = [PITCH * (i // 2) + 8 * (i % 2) for i in range(16)]
    return jnp.concatenate([ref[lead, start : start + 8, :] for start in starts], 0)


def spread(ref, lead, value):
    for i in range(16):
        start = PITCH * (i // 2) + 8 * (i % 2)
        ref[lead, start : start + 8, :] = value[8 * i : 8 * i + 8]


def factor(cells, first, coef_ref, tree_ref, head_ref, plane):
    row = sub_iota()
    last = row == 7
    faces = [0.5 * (cells[t] + cells[t + 1]) for t in range(SEG - 1)]
    faces.append(0.5 * (cells[SEG - 1] + ahead(cells[0], 1)))
    leak_l = 1.0 + jnp.where(jnp.logical_and(row == 0, first), 0.5 * cells[0], 0.0)
    g = faces[0]
    leak_r = jnp.ones_like(g)
    for t in range(1, SEG):
        f = faces[t]
        inv = 1.0 / (g + f + leak_r)
        a = g * inv
        b = f * inv
        if t == SEG - 1:
            inv = jnp.where(last, 0.0, inv)
            g = jnp.where(last, g, a * f)
            a = jnp.where(last, 0.0, a)
            b = jnp.where(last, 1.0, b)
            leak_l = leak_l + a * leak_r
            leak_r = b * leak_r
        else:
            g = a * f
            leak_l = leak_l + a * leak_r
            leak_r = 1.0 + b * leak_r
        coef_ref[plane, 0, t] = a
        coef_ref[plane, 1, t] = b
        coef_ref[plane, 2, t] = inv
    for level in range(3):
        count = 1 << level
        g_next = ahead(g, count)
        leak = leak_r + ahead(leak_l, count)
        inv = 1.0 / (g + g_next + leak)
        a = g * inv
        b = g_next * inv
        g = a * g_next
        leak_l = leak_l + a * leak
        leak_r = ahead(leak_r, count) + b * leak
        tree_ref[plane, level, 0] = a
        tree_ref[plane, level, 1] = b
        tree_ref[plane, level, 2] = inv
    if head_ref is None:
        return
    for base, value in ((ROW_G, g), (ROW_EL, leak_l), (ROW_ER, leak_r)):
        head_ref[base + plane : base + plane + 1, :] = value[0:1]
    head_ref[ROW_DHI + plane : ROW_DHI + plane + 1, :] = cells[SEG - 1][7:8]
    head_ref[ROW_DLO + plane : ROW_DLO + plane + 1, :] = cells[0][0:1]


def condense(sources, coef_ref, tree_ref, q_ref, qtree_ref, plane, comp):
    k = comp * PLANES + plane
    left = sources[0]
    right = sources[1]
    for t in range(1, SEG):
        q_ref[k, t] = coef_ref[plane, 2, t] * right
        left = left + coef_ref[plane, 0, t] * right
        right = coef_ref[plane, 1, t] * right
        if t < SEG - 1:
            right = right + sources[t + 1]
    for level in range(3):
        count = 1 << level
        j = right + ahead(left, count)
        left = left + tree_ref[plane, level, 0] * j
        right = ahead(right, count) + tree_ref[plane, level, 1] * j
        qtree_ref[k, level] = tree_ref[plane, level, 2] * j
    return left, right


def unfold(low, high, coef_ref, tree_ref, q_ref, qtree_ref, plane, comp, store):
    k = comp * PLANES + plane
    row = sub_iota()

    def mid(level, lo, hi):
        return (
            tree_ref[plane, level, 0] * lo
            + tree_ref[plane, level, 1] * hi
            + qtree_ref[k, level]
        )

    for level in (2, 1, 0):
        count = 1 << level
        between = mid(level, low, high)
        late = (row & count) != 0
        low = jnp.where(late, after(between, count), low)
        high = jnp.where(late, after(high, count), between)
    store(0, low)
    cell = high
    for t in range(SEG - 1, 0, -1):
        cell = (
            coef_ref[plane, 0, t] * low
            + q_ref[k, t]
            + coef_ref[plane, 1, t] * cell
        )
        store(t, cell)


def send_row(out_ref, rows, which, count, value):
    value = jnp.broadcast_to(value[0:1], (8, LANES))
    for half in range(count // 8):
        out_ref[pl.ds(8 * half * rows + which, 8, stride=rows), :] = value


def reader(got_ref, rows, me):
    turn = me & 7
    back = (8 - turn) & 7
    same = (sub_iota() < 8 - turn) == (me < 8)

    def read(which):
        low, high = (
            pltpu.roll(got_ref[pl.ds(8 * half * rows + which, 8, stride=rows), :], back, 0)
            for half in (0, 1)
        )
        return jnp.where(same, low, high), jnp.where(same, high, low)

    return read


def cyclic(me, half, count):
    return (me + 8 * half + sub_iota()) & (count - 1)


def solve_ring(blocks, me, count):
    halves = []
    for g, leak_l, leak_r, currents in blocks:
        levels = []
        for level in range(3):
            step = 1 << level
            g_next = ahead(g, step)
            leak = leak_r + ahead(leak_l, step)
            inv = 1.0 / (g + g_next + leak)
            a = g * inv
            b = g_next * inv
            g = a * g_next
            leak_l = leak_l + a * leak
            leak_r = ahead(leak_r, step) + b * leak
            levels.append((a, b, inv))
        merged = []
        for left, right in currents:
            terms = []
            for level in range(3):
                step = 1 << level
                a, b, inv = levels[level]
                j = right + ahead(left, step)
                left = left + a * j
                right = ahead(right, step) + b * j
                terms.append(inv * j)
            merged.append((left, right, terms))
        halves.append((g, leak_l, leak_r, levels, merged))
    g, leak_l, leak_r, levels, merged = halves[0]
    g_next, leak_l_next, leak_r_next, _, merged_next = halves[1]
    leak = leak_r + leak_l_next
    inv = 1.0 / (g + g_next + leak)
    a = g * inv
    b = g_next * inv
    total = 1.0 / (leak_l + a * leak + leak_r_next + b * leak)
    ends = []
    for comp in range(COMPS):
        left, right, terms = merged[comp]
        left_next, right_next, _ = merged_next[comp]
        j = right + left_next
        first = (left + a * j + right_next + b * j) * total
        high = (a + b) * first + inv * j
        for level in (2, 1, 0):
            high = levels[level][0] * first + levels[level][1] * high + terms[level]
        ends.append((first, jnp.where(me == count - 1, 0.0, high)))
    return ends


def solve_x(read, me, count, plane):
    row = sub_iota()

    def both(which):
        return read(which + plane)

    def before(pair, half):
        return jnp.where(row == 0, after(pair[1 - half], 1), after(pair[half], 1))

    def beyond(pair, half):
        return jnp.where(row == 7, ahead(pair[1 - half], 1), ahead(pair[half], 1))

    conduct = both(ROW_G)
    leaks_l = both(ROW_EL)
    leaks_r = both(ROW_ER)
    last_faces = both(ROW_DHI)
    first_faces = both(ROW_DLO)
    lefts = [both(ROW_JL + comp * PLANES) for comp in range(COMPS)]
    rights = [both(ROW_JR + comp * PLANES) for comp in range(COMPS)]
    low_cells = [both(ROW_VLO + comp * PLANES) for comp in range(COMPS)]
    high_cells = [both(ROW_VHI + comp * PLANES) for comp in range(COMPS)]
    blocks = []
    own = None
    for half in (0, 1):
        place = cyclic(me, half, count)
        wall = place == count - 1
        g = conduct[half]
        leak_l = leaks_l[half]
        leak_r = leaks_r[half]
        f = 0.5 * (last_faces[half] + jnp.where(wall, 0.0, beyond(first_faces, half)))
        inv = 1.0 / (g + f + leak_r)
        a = g * inv
        b = f * inv
        through = a * f
        leak_l = leak_l + a * leak_r
        leak_l = jnp.where(wall, leak_l + through, leak_l)
        up_lo = jnp.where(place == 0, 0.0, HALF * low_cells[0][half])
        up_hi = jnp.where(wall, 0.0, HALF * high_cells[0][half])
        b_cut = jnp.where(wall, 0.0, b)
        currents = []
        terms = []
        for comp in range(COMPS):
            left = lefts[comp][half] + up_lo * before(high_cells[comp], half)
            right = rights[comp][half] - up_hi * beyond(low_cells[comp], half)
            terms.append(inv * right)
            currents.append((left + a * right, b_cut * right))
        if half == 0:
            own = (a, b, terms)
        blocks.append((jnp.where(wall, 0.0, through), leak_l, b_cut * leak_r, currents))
    ends = solve_ring(blocks, me, count)
    a, b, terms = own
    return [
        (first, a * first + b * high + terms[comp]) for comp, (first, high) in enumerate(ends)
    ]


def solve_y(read, own_ref, me, count, plane):
    def own(which):
        return own_ref[which + plane : which + plane + 1, :]

    g, leak_l, leak_r = (read(which + plane) for which in (ROW_G, ROW_EL, ROW_ER))
    lefts = [read(Y_JL + comp * PLANES + plane) for comp in range(COMPS)]
    rights = [read(Y_JR + comp * PLANES + plane) for comp in range(COMPS)]
    blocks = [
        (
            g[half],
            leak_l[half],
            leak_r[half],
            [(lefts[comp][half], rights[comp][half]) for comp in range(COMPS)],
        )
        for half in (0, 1)
    ]
    ends = solve_ring(blocks, me, count)
    return [
        (first, own(OWN_A) * first + own(OWN_B) * high + own(OWN_Q + comp * PLANES))
        for comp, (first, high) in enumerate(ends)
    ]


def by_parity(even, odd):
    return jnp.where(lax.axis_index("gy") % 2 == 0, even, odd)


def edges_kernel(velocity_ref, diffusion_ref, low_ref, high_ref, near_ref, far_ref, v_ref, d_ref,
                 turn_ref, sem):
    copies = [
        pltpu.make_async_copy(velocity_ref, v_ref, sem.at[0]),
        pltpu.make_async_copy(diffusion_ref, d_ref, sem.at[1]),
    ]
    for copy in copies:
        copy.start()
    for copy in copies:
        copy.wait()
    for k in range(COMPS * PLANES + PLANES):
        if k < COMPS * PLANES:
            comp, plane = divmod(k, PLANES)
            turned = jnp.transpose(v_ref[comp, plane])
        else:
            turned = jnp.transpose(d_ref[k - 6])
            turn_ref[k - 6] = turned
        low = turned[0:1]
        high = turned[LANES - 1 : LANES]
        low_ref[k : k + 1, :] = low
        high_ref[k : k + 1, :] = high
        near_ref[k : k + 1, :] = by_parity(high, low)
        far_ref[k : k + 1, :] = by_parity(low, high)


def matrix_kernel(diffusion_ref, turn_ref, low_ref, high_ref, cx_ref, tx_ref, hx_ref, cy_ref, ty_ref,
                  hy_ref, cp_ref, tp_ref, vp_ref, edge_ref, pack_ref):
    first_x = lax.axis_index("gx") == 0
    first_y = lax.axis_index("gy") == 0
    edge_ref[...] = jnp.zeros((2, LANES, LANES), f32)
    for i, base in enumerate((2, 6)):
        for k in range(COMPS * PLANES):
            line = base + k % PLANES
            edge_ref[i, k : k + 1, :] = low_ref[line : line + 1, :]
            edge_ref[i, 8 + k : 9 + k, :] = high_ref[line : line + 1, :]
    for i in range(2):
        pack_ref[i] = jnp.transpose(edge_ref[i])
    for t in range(SEG):
        vp_ref[t] = strided(pack_ref, 0, t)
    for plane in range(PLANES):
        cells = [strided(diffusion_ref, plane, t) for t in range(SEG)]
        factor(cells, first_x, cx_ref, tx_ref, hx_ref, plane)
        cells = [strided(turn_ref, plane, t) for t in range(SEG)]
        factor(cells, first_y, cy_ref, ty_ref, hy_ref, plane)
    cells = [strided(pack_ref, 1, t) for t in range(SEG)]
    factor(cells, first_x, cp_ref, tp_ref, None, 0)
    for ref in (hx_ref, hy_ref):
        ref[ROW_VLO : ROW_VLO + 6, :] = jnp.zeros((6, LANES), f32)


def source_kernel(velocity_ref, coef_ref, tree_ref, head_ref, page_ref, q_ref, qtree_ref):
    row = sub_iota()
    lane = lane_iota()
    page_ref[0:16, :] = head_ref[...]
    page_ref[ROWS_X:, :] = jnp.zeros((40 - ROWS_X, LANES), f32)
    for plane in range(PLANES):
        cells = [
            [velocity_ref[comp, plane, pl.ds(t, 8, stride=SEG), :] for t in range(SEG)]
            for comp in range(COMPS)
        ]
        for comp in range(COMPS):
            k = comp * PLANES + plane
            own = cells[comp]
            sources = []
            for t in range(SEG):
                if t < SEG - 1:
                    fore = own[t + 1]
                else:
                    fore = jnp.where(row == 7, 0.0, ahead(own[0], 1))
                if t > 0:
                    back = own[t - 1]
                else:
                    back = jnp.where(row == 0, 0.0, after(own[SEG - 1], 1))
                right = jnp.where(lane == LANES - 1, 0.0, pltpu.roll(own[t], LANES - 1, 1))
                left = jnp.where(lane == 0, 0.0, pltpu.roll(own[t], 1, 1))
                sources.append(
                    own[t]
                    - HALF * (cells[0][t] * (fore - back) + cells[1][t] * (right - left))
                )
            left, right = condense(sources, coef_ref, tree_ref, q_ref, qtree_ref, plane, comp)
            page_ref[ROW_JL + k : ROW_JL + k + 1, :] = left[0:1]
            page_ref[ROW_JR + k : ROW_JR + k + 1, :] = right[0:1]
            page_ref[ROW_VLO + k : ROW_VLO + k + 1, :] = own[0][0:1]
            page_ref[ROW_VHI + k : ROW_VHI + k + 1, :] = own[SEG - 1][7:8]


def halo_kernel(count, from_near_ref, from_far_ref, vp_ref, coef_ref, tree_ref, page_ref, out_ref,
                q_ref, qtree_ref, edge_ref, halo_ref):
    me_y = lax.axis_index("gy")
    count_y = lax.axis_size("gy")
    row = sub_iota()
    lane = lane_iota()
    near = from_near_ref[...]
    far = from_far_ref[...]
    edge_ref[0:8, :] = jnp.where(me_y == 0, 0.0, HALF * by_parity(far, near))
    edge_ref[8:16, :] = jnp.where(me_y == count_y - 1, 0.0, -HALF * by_parity(near, far))
    edge_ref[16:, :] = jnp.zeros((LANES - 16, LANES), f32)
    spread(halo_ref, 0, jnp.transpose(edge_ref[...]))
    sources = [
        vp_ref[t] * halo_ref[0, segment(t), :]
        for t in range(SEG)
    ]
    ends = condense(sources, coef_ref, tree_ref, q_ref, qtree_ref, 0, 0)
    done = {}
    for base, value in zip((ROW_JL, ROW_JR), ends):
        value = jnp.broadcast_to(value[0:1], (8, LANES))
        low = jnp.sum(jnp.where(lane == row, value, 0.0), axis=1, keepdims=True)
        high = jnp.sum(jnp.where(lane == row + 8, value, 0.0), axis=1, keepdims=True)
        extra = jnp.where(lane == 0, low, jnp.where(lane == LANES - 1, high, 0.0))
        for k in range(COMPS * PLANES):
            done[base + k] = page_ref[base + k : base + k + 1, :] + extra[k : k + 1]
    for which in range(ROWS_X):
        value = done.get(which)
        if value is None:
            value = page_ref[which : which + 1, :]
        send_row(out_ref, ROWS_X, which, count, value)


def middle_kernel(count_x, count_y, got_ref, from_near_ref, from_far_ref, cx_ref, tx_ref, qx_ref, qtx_ref, cy_ref,
                  ty_ref, hy_ref, cp_ref, tp_ref, qp_ref, qtp_ref, out_ref, q_ref, qtree_ref, own_ref,
                  plane_ref, turn_ref, pack_ref, extra_ref):
    me = lax.axis_index("gx")

    def store_pack(t, value):
        pack_ref[0, segment(t), :] = value

    nothing = jnp.zeros((8, LANES), f32)
    unfold(nothing, nothing, cp_ref, tp_ref, qp_ref, qtp_ref, 0, 0, store_pack)
    extra_ref[...] = jnp.transpose(natural(pack_ref, 0))
    wall = lax.axis_index("gy") == count_y - 1
    read = reader(got_ref, ROWS_X, me)
    own_ref[10:16, :] = jnp.zeros((6, LANES), f32)
    values = {}
    for plane in range(PLANES):

        def head(which):
            return hy_ref[which + plane : which + plane + 1, :]

        g = head(ROW_G)
        leak_r = head(ROW_ER)
        line = slice(6 + plane, 7 + plane)
        beyond = by_parity(from_near_ref[line, :], from_far_ref[line, :])
        f = 0.5 * (head(ROW_DHI) + jnp.where(wall, 0.0, beyond))
        inv = 1.0 / (g + f + leak_r)
        a = g * inv
        b = f * inv
        through = a * f
        b_cut = jnp.where(wall, 0.0, b)
        own_ref[OWN_A + plane : OWN_A + plane + 1, :] = a
        own_ref[OWN_B + plane : OWN_B + plane + 1, :] = b
        values[ROW_G + plane] = jnp.where(wall, 0.0, through)
        leak_l = head(ROW_EL) + a * leak_r
        values[ROW_EL + plane] = jnp.where(wall, leak_l + through, leak_l)
        values[ROW_ER + plane] = b_cut * leak_r
        ends = solve_x(read, me, count_x, plane)
        for comp in range(COMPS):
            k = comp * PLANES + plane
            low, high = ends[comp]

            def store(t, value):
                plane_ref[k, segment(t), :] = value

            unfold(low, high, cx_ref, tx_ref, qx_ref, qtx_ref, plane, comp, store)
            turned = jnp.transpose(natural(plane_ref, k))
            spread(turn_ref, k, turned)
            turn_ref[k, 0:1, :] = turned[0:1] + extra_ref[k : k + 1, :]
            final = PITCH * 7 + SEG - 1
            turn_ref[k, final : final + 1, :] = turned[LANES - 1 :] + extra_ref[8 + k : 9 + k, :]
            sources = [turn_ref[k, segment(t), :] for t in range(SEG)]
            left, right = condense(sources, cy_ref, ty_ref, q_ref, qtree_ref, plane, comp)
            right = right[0:1]
            own_ref[OWN_Q + k : OWN_Q + k + 1, :] = inv * right
            values[Y_JL + k] = left[0:1] + a * right
            values[Y_JR + k] = b_cut * right
    for which, value in values.items():
        send_row(out_ref, ROWS_Y, which, count_y, value)


def final_kernel(count, got_ref, own_ref, coef_ref, tree_ref, q_ref, qtree_ref, out_ref, plane_ref,
                 turn_ref, sem):
    me = lax.axis_index("gy")
    read = reader(got_ref, ROWS_Y, me)
    copies = []
    for plane in range(PLANES):
        ends = solve_y(read, own_ref, me, count, plane)
        for comp in range(COMPS):
            k = comp * PLANES + plane
            low, high = ends[comp]

            def store(t, value):
                plane_ref[k, segment(t), :] = value

            unfold(low, high, coef_ref, tree_ref, q_ref, qtree_ref, plane, comp, store)
            turn_ref[k] = jnp.transpose(natural(plane_ref, k))
            copy = pltpu.make_async_copy(turn_ref.at[k], out_ref.at[comp, plane], sem.at[k])
            copy.start()
            copies.append(copy)
    for copy in copies:
        copy.wait()


def shape(*dims):
    return jax.ShapeDtypeStruct(dims, f32)


def call(kernel, ins, outs, scratch, cost, *args):
    return pl.pallas_call(
        kernel,
        out_shape=tuple(o for o, _ in outs),
        in_specs=[pl.BlockSpec(memory_space=m) for m in ins],
        out_specs=tuple(pl.BlockSpec(memory_space=m) for _, m in outs),
        scratch_shapes=scratch,
        cost_estimate=pl.CostEstimate(flops=cost, bytes_accessed=1 << 19, transcendentals=0),
        compiler_params=pltpu.CompilerParams(vmem_limit_bytes=8 << 20),
    )(*args)


def share(sent, axis):
    count = lax.axis_size(axis)
    got = lax.all_to_all(sent.reshape(count, -1, 2, LANES), axis, 0, 0)
    return got.reshape(-1, LANES)


def local(velocity, diffusion):
    count_x = lax.axis_size("gx")
    count_y = lax.axis_size("gy")
    tile = (8, LANES)
    n = COMPS * PLANES
    low, high, near, far, cells, diff, turned = call(
        edges_kernel,
        (HBM, HBM),
        [
            (shape(*tile), VMEM),
            (shape(*tile), VMEM),
            (shape(*tile), VMEM),
            (shape(*tile), VMEM),
            (shape(COMPS, PLANES, LANES, LANES), VMEM),
            (shape(PLANES, LANES, LANES), VMEM),
            (shape(PLANES, LANES, LANES), VMEM),
        ],
        [pltpu.SemaphoreType.DMA((2,))],
        1 << 17,
        pltpu.with_memory_space_constraint(velocity, HBM),
        pltpu.with_memory_space_constraint(diffusion, HBM),
    )
    ring = range(count_y)
    from_far = lax.ppermute(far, "gy", [(i, (i - 1 + 2 * (i % 2)) % count_y) for i in ring])
    from_near = lax.ppermute(near, "gy", [(i, i ^ 1) for i in ring])
    coef = (shape(PLANES, 3, SEG, *tile), VMEM)
    tree = (shape(PLANES, 3, 3, *tile), VMEM)
    head = (shape(16, LANES), VMEM)
    q_all = (shape(n, SEG, *tile), VMEM)
    q_tree = (shape(n, 3, *tile), VMEM)
    block = VMEM((n, LANES, LANES), f32)
    pitched = VMEM((n, 8 * PITCH, LANES), f32)
    square = VMEM((LANES, LANES), f32)
    pair = VMEM((PLANES, LANES, LANES), f32)
    coef_pack = (shape(1, 3, SEG, *tile), VMEM)
    tree_pack = (shape(1, 3, 3, *tile), VMEM)
    cx, tx, hx, cy, ty, hy, cp, tp, vp = call(
        matrix_kernel,
        (VMEM,) * 4,
        [coef, tree, head] * 2 + [coef_pack, tree_pack, (shape(SEG, *tile), VMEM)],
        [pair, pair],
        1 << 21,
        diff, turned, low, high,
    )
    page, qx, qtx = call(
        source_kernel,
        (VMEM,) * 4,
        [(shape(40, LANES), VMEM), q_all, q_tree],
        [],
        1 << 22,
        cells, cx, tx, hx,
    )
    sent, qp, qtp = call(
        partial(halo_kernel, count_x),
        (VMEM,) * 6,
        [
            (shape(count_x * ROWS_X, LANES), VMEM),
            (shape(1, SEG, *tile), VMEM),
            (shape(1, 3, *tile), VMEM),
        ],
        [square, VMEM((1, 8 * PITCH, LANES), f32)],
        1 << 18,
        from_near, from_far, vp, cp, tp, page,
    )
    got = share(sent, "gx")
    sent, qy, qty, own = call(
        partial(middle_kernel, count_x, count_y),
        (VMEM,) * 14,
        [(shape(count_y * ROWS_Y, LANES), VMEM), q_all, q_tree, head],
        [pitched, pitched, VMEM((1, 8 * PITCH, LANES), f32), square],
        1 << 22,
        got, from_near, from_far, cx, tx, qx, qtx, cy, ty, hy, cp, tp, qp, qtp,
    )
    got = share(sent, "gy")
    (result,) = call(
        partial(final_kernel, count_y),
        (VMEM,) * 6,
        [(shape(COMPS, PLANES, LANES, LANES), HBM)],
        [
            pitched,
            block,
            pltpu.SemaphoreType.DMA((n,)),
        ],
        1 << 22,
        got, own, cy, ty, qy, qty,
    )
    return result


def solution(mesh):
    in_specs = (P(None, None, "gx", "gy"), P(None, "gx", "gy"))
    out_specs = P(None, None, "gx", "gy")
    return jax.shard_map(local, mesh=mesh, in_specs=in_specs, out_specs=out_specs, check_vma=False)
```

```python
from functools import partial

import jax
import jax.numpy as jnp
from jax import lax
from jax.experimental import pallas as pl
from jax.experimental.pallas import tpu as pltpu
from jax.sharding import PartitionSpec as P


COURANT = 0.25
HALF = 0.5 * COURANT
SEG = 16
PLANES = 2
COMPS = 3
LANES = 128
PITCH = 18
ROWS_X = 34
ROWS_Y = 18
ROW_G, ROW_EL, ROW_ER, ROW_DHI, ROW_VLO, ROW_DLO = 0, 2, 4, 6, 8, 14
ROW_JL, ROW_JR, ROW_VHI = 16, 22, 28
Y_JL, Y_JR = 6, 12
OWN_A, OWN_B, OWN_Q = 0, 2, 4

ORDER_X = [6, 11, 15, 0, 7, 9, 12, 3, 4, 8, 13, 1, 5, 10, 14, 2]
ORDER_Y = [11, 8, 2, 9, 7, 5, 6, 13, 14, 4, 15, 12, 10, 0, 3, 1]

f32 = jnp.float32
VMEM = pltpu.VMEM
HBM = pltpu.HBM


def sub_iota():
    return lax.broadcasted_iota(jnp.int32, (8, LANES), 0)


def lane_iota():
    return lax.broadcasted_iota(jnp.int32, (8, LANES), 1)


def ahead(x, count):
    return pltpu.roll(x, 8 - count, 0)


def after(x, count):
    return pltpu.roll(x, count, 0)


def strided(ref, lead, t):
    return ref[lead, pl.ds(t, 8, stride=SEG), :]


def segment(t):
    return pl.ds(t, 8, stride=PITCH)


def natural(ref, lead):
    starts = [PITCH * (i // 2) + 8 * (i % 2) for i in range(16)]
    return jnp.concatenate([ref[lead, start : start + 8, :] for start in starts], 0)


def spread(ref, lead, value):
    for i in range(16):
        start = PITCH * (i // 2) + 8 * (i % 2)
        ref[lead, start : start + 8, :] = value[8 * i : 8 * i + 8]


def factor(cells, first, coef_ref, tree_ref, head_ref, plane):
    row = sub_iota()
    last = row == 7
    faces = [0.5 * (cells[t] + cells[t + 1]) for t in range(SEG - 1)]
    faces.append(0.5 * (cells[SEG - 1] + ahead(cells[0], 1)))
    leak_l = 1.0 + jnp.where(jnp.logical_and(row == 0, first), 0.5 * cells[0], 0.0)
    g = faces[0]
    leak_r = jnp.ones_like(g)
    for t in range(1, SEG):
        f = faces[t]
        inv = 1.0 / (g + f + leak_r)
        a = g * inv
        b = f * inv
        if t == SEG - 1:
            inv = jnp.where(last, 0.0, inv)
            g = jnp.where(last, g, a * f)
            a = jnp.where(last, 0.0, a)
            b = jnp.where(last, 1.0, b)
            leak_l = leak_l + a * leak_r
            leak_r = b * leak_r
        else:
            g = a * f
            leak_l = leak_l + a * leak_r
            leak_r = 1.0 + b * leak_r
        coef_ref[plane, 0, t] = a
        coef_ref[plane, 1, t] = b
        coef_ref[plane, 2, t] = inv
    for level in range(3):
        count = 1 << level
        g_next = ahead(g, count)
        leak = leak_r + ahead(leak_l, count)
        inv = 1.0 / (g + g_next + leak)
        a = g * inv
        b = g_next * inv
        g = a * g_next
        leak_l = leak_l + a * leak
        leak_r = ahead(leak_r, count) + b * leak
        tree_ref[plane, level, 0] = a
        tree_ref[plane, level, 1] = b
        tree_ref[plane, level, 2] = inv
    if head_ref is None:
        return
    for base, value in ((ROW_G, g), (ROW_EL, leak_l), (ROW_ER, leak_r)):
        head_ref[base + plane : base + plane + 1, :] = value[0:1]
    head_ref[ROW_DHI + plane : ROW_DHI + plane + 1, :] = cells[SEG - 1][7:8]
    head_ref[ROW_DLO + plane : ROW_DLO + plane + 1, :] = cells[0][0:1]


def condense(sources, coef_ref, tree_ref, q_ref, qtree_ref, plane, comp):
    k = comp * PLANES + plane
    left = sources[0]
    right = sources[1]
    for t in range(1, SEG):
        q_ref[k, t] = coef_ref[plane, 2, t] * right
        left = left + coef_ref[plane, 0, t] * right
        right = coef_ref[plane, 1, t] * right
        if t < SEG - 1:
            right = right + sources[t + 1]
    for level in range(3):
        count = 1 << level
        j = right + ahead(left, count)
        left = left + tree_ref[plane, level, 0] * j
        right = ahead(right, count) + tree_ref[plane, level, 1] * j
        qtree_ref[k, level] = tree_ref[plane, level, 2] * j
    return left, right


def unfold(low, high, coef_ref, tree_ref, q_ref, qtree_ref, plane, comp, store):
    k = comp * PLANES + plane
    row = sub_iota()

    def mid(level, lo, hi):
        return (
            tree_ref[plane, level, 0] * lo
            + tree_ref[plane, level, 1] * hi
            + qtree_ref[k, level]
        )

    for level in (2, 1, 0):
        count = 1 << level
        between = mid(level, low, high)
        late = (row & count) != 0
        low = jnp.where(late, after(between, count), low)
        high = jnp.where(late, after(high, count), between)
    store(0, low)
    cell = high
    for t in range(SEG - 1, 0, -1):
        cell = (
            coef_ref[plane, 0, t] * low
            + q_ref[k, t]
            + coef_ref[plane, 1, t] * cell
        )
        store(t, cell)


def send_row(out_ref, rows, which, count, value):
    value = jnp.broadcast_to(value[0:1], (8, LANES))
    for half in range(count // 8):
        out_ref[pl.ds(8 * half * rows + which, 8, stride=rows), :] = value


def reader(got_ref, ring_ref, rows, order, me):
    count = len(order)
    for i, source in enumerate(order):
        base = ((source - me + count) & (count - 1)) * rows
        for start in range(0, rows, 8):
            size = min(8, rows - start)
            piece = got_ref[rows * i + start : rows * i + start + size, :]
            ring_ref[pl.ds(base + start, size), :] = piece

    def read(which):
        return tuple(
            ring_ref[pl.ds(8 * half * rows + which, 8, stride=rows), :] for half in (0, 1)
        )

    return read


def cyclic(me, half, count):
    return (me + 8 * half + sub_iota()) & (count - 1)


def solve_ring(blocks, me, count):
    halves = []
    for g, leak_l, leak_r, currents in blocks:
        levels = []
        for level in range(3):
            step = 1 << level
            g_next = ahead(g, step)
            leak = leak_r + ahead(leak_l, step)
            inv = 1.0 / (g + g_next + leak)
            a = g * inv
            b = g_next * inv
            g = a * g_next
            leak_l = leak_l + a * leak
            leak_r = ahead(leak_r, step) + b * leak
            levels.append((a, b, inv))
        merged = []
        for left, right in currents:
            terms = []
            for level in range(3):
                step = 1 << level
                a, b, inv = levels[level]
                j = right + ahead(left, step)
                left = left + a * j
                right = ahead(right, step) + b * j
                terms.append(inv * j)
            merged.append((left, right, terms))
        halves.append((g, leak_l, leak_r, levels, merged))
    g, leak_l, leak_r, levels, merged = halves[0]
    g_next, leak_l_next, leak_r_next, _, merged_next = halves[1]
    leak = leak_r + leak_l_next
    inv = 1.0 / (g + g_next + leak)
    a = g * inv
    b = g_next * inv
    total = 1.0 / (leak_l + a * leak + leak_r_next + b * leak)
    ends = []
    for comp in range(COMPS):
        left, right, terms = merged[comp]
        left_next, right_next, _ = merged_next[comp]
        j = right + left_next
        first = (left + a * j + right_next + b * j) * total
        high = (a + b) * first + inv * j
        for level in (2, 1, 0):
            high = levels[level][0] * first + levels[level][1] * high + terms[level]
        ends.append((first, jnp.where(me == count - 1, 0.0, high)))
    return ends


def solve_x(read, me, count, plane):
    row = sub_iota()

    def both(which):
        return read(which + plane)

    def before(pair, half):
        return jnp.where(row == 0, after(pair[1 - half], 1), after(pair[half], 1))

    def beyond(pair, half):
        return jnp.where(row == 7, ahead(pair[1 - half], 1), ahead(pair[half], 1))

    conduct = both(ROW_G)
    leaks_l = both(ROW_EL)
    leaks_r = both(ROW_ER)
    last_faces = both(ROW_DHI)
    first_faces = both(ROW_DLO)
    lefts = [both(ROW_JL + comp * PLANES) for comp in range(COMPS)]
    rights = [both(ROW_JR + comp * PLANES) for comp in range(COMPS)]
    low_cells = [both(ROW_VLO + comp * PLANES) for comp in range(COMPS)]
    high_cells = [both(ROW_VHI + comp * PLANES) for comp in range(COMPS)]
    blocks = []
    own = None
    for half in (0, 1):
        place = cyclic(me, half, count)
        wall = place == count - 1
        g = conduct[half]
        leak_l = leaks_l[half]
        leak_r = leaks_r[half]
        f = 0.5 * (last_faces[half] + jnp.where(wall, 0.0, beyond(first_faces, half)))
        inv = 1.0 / (g + f + leak_r)
        a = g * inv
        b = f * inv
        through = a * f
        leak_l = leak_l + a * leak_r
        leak_l = jnp.where(wall, leak_l + through, leak_l)
        up_lo = jnp.where(place == 0, 0.0, HALF * low_cells[0][half])
        up_hi = jnp.where(wall, 0.0, HALF * high_cells[0][half])
        b_cut = jnp.where(wall, 0.0, b)
        currents = []
        terms = []
        for comp in range(COMPS):
            left = lefts[comp][half] + up_lo * before(high_cells[comp], half)
            right = rights[comp][half] - up_hi * beyond(low_cells[comp], half)
            terms.append(inv * right)
            currents.append((left + a * right, b_cut * right))
        if half == 0:
            own = (a, b, terms)
        blocks.append((jnp.where(wall, 0.0, through), leak_l, b_cut * leak_r, currents))
    ends = solve_ring(blocks, me, count)
    a, b, terms = own
    return [
        (first, a * first + b * high + terms[comp]) for comp, (first, high) in enumerate(ends)
    ]


def solve_y(read, own_ref, me, count, plane):
    def own(which):
        return own_ref[which + plane : which + plane + 1, :]

    g, leak_l, leak_r = (read(which + plane) for which in (ROW_G, ROW_EL, ROW_ER))
    lefts = [read(Y_JL + comp * PLANES + plane) for comp in range(COMPS)]
    rights = [read(Y_JR + comp * PLANES + plane) for comp in range(COMPS)]
    blocks = [
        (
            g[half],
            leak_l[half],
            leak_r[half],
            [(lefts[comp][half], rights[comp][half]) for comp in range(COMPS)],
        )
        for half in (0, 1)
    ]
    ends = solve_ring(blocks, me, count)
    return [
        (first, own(OWN_A) * first + own(OWN_B) * high + own(OWN_Q + comp * PLANES))
        for comp, (first, high) in enumerate(ends)
    ]


def by_parity(even, odd):
    return jnp.where(lax.axis_index("gy") % 2 == 0, even, odd)


def edges_kernel(velocity_ref, diffusion_ref, low_ref, high_ref, near_ref, far_ref, v_ref, d_ref,
                 turn_ref, sem):
    copies = [
        pltpu.make_async_copy(velocity_ref, v_ref, sem.at[0]),
        pltpu.make_async_copy(diffusion_ref, d_ref, sem.at[1]),
    ]
    for copy in copies:
        copy.start()
    for copy in copies:
        copy.wait()
    for k in range(COMPS * PLANES + PLANES):
        if k < COMPS * PLANES:
            comp, plane = divmod(k, PLANES)
            turned = jnp.transpose(v_ref[comp, plane])
        else:
            turned = jnp.transpose(d_ref[k - 6])
            turn_ref[k - 6] = turned
        low = turned[0:1]
        high = turned[LANES - 1 : LANES]
        low_ref[k : k + 1, :] = low
        high_ref[k : k + 1, :] = high
        near_ref[k : k + 1, :] = by_parity(high, low)
        far_ref[k : k + 1, :] = by_parity(low, high)


def matrix_kernel(diffusion_ref, turn_ref, low_ref, high_ref, cx_ref, tx_ref, hx_ref, cy_ref, ty_ref,
                  hy_ref, cp_ref, tp_ref, vp_ref, edge_ref, pack_ref):
    first_x = lax.axis_index("gx") == 0
    first_y = lax.axis_index("gy") == 0
    edge_ref[...] = jnp.zeros((2, LANES, LANES), f32)
    for i, base in enumerate((2, 6)):
        for k in range(COMPS * PLANES):
            line = base + k % PLANES
            edge_ref[i, k : k + 1, :] = low_ref[line : line + 1, :]
            edge_ref[i, 8 + k : 9 + k, :] = high_ref[line : line + 1, :]
    for i in range(2):
        pack_ref[i] = jnp.transpose(edge_ref[i])
    for t in range(SEG):
        vp_ref[t] = strided(pack_ref, 0, t)
    for plane in range(PLANES):
        cells = [strided(diffusion_ref, plane, t) for t in range(SEG)]
        factor(cells, first_x, cx_ref, tx_ref, hx_ref, plane)
        cells = [strided(turn_ref, plane, t) for t in range(SEG)]
        factor(cells, first_y, cy_ref, ty_ref, hy_ref, plane)
    cells = [strided(pack_ref, 1, t) for t in range(SEG)]
    factor(cells, first_x, cp_ref, tp_ref, None, 0)
    for ref in (hx_ref, hy_ref):
        ref[ROW_VLO : ROW_VLO + 6, :] = jnp.zeros((6, LANES), f32)


def source_kernel(velocity_ref, coef_ref, tree_ref, head_ref, page_ref, q_ref, qtree_ref):
    row = sub_iota()
    lane = lane_iota()
    page_ref[0:16, :] = head_ref[...]
    page_ref[ROWS_X:, :] = jnp.zeros((40 - ROWS_X, LANES), f32)
    for plane in range(PLANES):
        cells = [
            [velocity_ref[comp, plane, pl.ds(t, 8, stride=SEG), :] for t in range(SEG)]
            for comp in range(COMPS)
        ]
        for comp in range(COMPS):
            k = comp * PLANES + plane
            own = cells[comp]
            sources = []
            for t in range(SEG):
                if t < SEG - 1:
                    fore = own[t + 1]
                else:
                    fore = jnp.where(row == 7, 0.0, ahead(own[0], 1))
                if t > 0:
                    back = own[t - 1]
                else:
                    back = jnp.where(row == 0, 0.0, after(own[SEG - 1], 1))
                right = jnp.where(lane == LANES - 1, 0.0, pltpu.roll(own[t], LANES - 1, 1))
                left = jnp.where(lane == 0, 0.0, pltpu.roll(own[t], 1, 1))
                sources.append(
                    own[t]
                    - HALF * (cells[0][t] * (fore - back) + cells[1][t] * (right - left))
                )
            left, right = condense(sources, coef_ref, tree_ref, q_ref, qtree_ref, plane, comp)
            page_ref[ROW_JL + k : ROW_JL + k + 1, :] = left[0:1]
            page_ref[ROW_JR + k : ROW_JR + k + 1, :] = right[0:1]
            page_ref[ROW_VLO + k : ROW_VLO + k + 1, :] = own[0][0:1]
            page_ref[ROW_VHI + k : ROW_VHI + k + 1, :] = own[SEG - 1][7:8]


def halo_kernel(count, from_near_ref, from_far_ref, vp_ref, coef_ref, tree_ref, page_ref, out_ref,
                q_ref, qtree_ref, edge_ref, halo_ref):
    me_y = lax.axis_index("gy")
    count_y = lax.axis_size("gy")
    row = sub_iota()
    lane = lane_iota()
    near = from_near_ref[...]
    far = from_far_ref[...]
    edge_ref[0:8, :] = jnp.where(me_y == 0, 0.0, HALF * by_parity(far, near))
    edge_ref[8:16, :] = jnp.where(me_y == count_y - 1, 0.0, -HALF * by_parity(near, far))
    edge_ref[16:, :] = jnp.zeros((LANES - 16, LANES), f32)
    spread(halo_ref, 0, jnp.transpose(edge_ref[...]))
    sources = [
        vp_ref[t] * halo_ref[0, segment(t), :]
        for t in range(SEG)
    ]
    ends = condense(sources, coef_ref, tree_ref, q_ref, qtree_ref, 0, 0)
    done = {}
    for base, value in zip((ROW_JL, ROW_JR), ends):
        value = jnp.broadcast_to(value[0:1], (8, LANES))
        low = jnp.sum(jnp.where(lane == row, value, 0.0), axis=1, keepdims=True)
        high = jnp.sum(jnp.where(lane == row + 8, value, 0.0), axis=1, keepdims=True)
        extra = jnp.where(lane == 0, low, jnp.where(lane == LANES - 1, high, 0.0))
        for k in range(COMPS * PLANES):
            done[base + k] = page_ref[base + k : base + k + 1, :] + extra[k : k + 1]
    for which in range(ROWS_X):
        value = done.get(which)
        if value is None:
            value = page_ref[which : which + 1, :]
        send_row(out_ref, ROWS_X, which, count, value)


def middle_kernel(count_x, count_y, got_ref, from_near_ref, from_far_ref, cx_ref, tx_ref, qx_ref, qtx_ref, cy_ref,
                  ty_ref, hy_ref, cp_ref, tp_ref, qp_ref, qtp_ref, out_ref, q_ref, qtree_ref, own_ref,
                  plane_ref, turn_ref, pack_ref, extra_ref, ring_ref):
    me = lax.axis_index("gx")

    def store_pack(t, value):
        pack_ref[0, segment(t), :] = value

    nothing = jnp.zeros((8, LANES), f32)
    unfold(nothing, nothing, cp_ref, tp_ref, qp_ref, qtp_ref, 0, 0, store_pack)
    extra_ref[...] = jnp.transpose(natural(pack_ref, 0))
    wall = lax.axis_index("gy") == count_y - 1
    read = reader(got_ref, ring_ref, ROWS_X, ORDER_X, me)
    own_ref[10:16, :] = jnp.zeros((6, LANES), f32)
    values = {}
    for plane in range(PLANES):

        def head(which):
            return hy_ref[which + plane : which + plane + 1, :]

        g = head(ROW_G)
        leak_r = head(ROW_ER)
        line = slice(6 + plane, 7 + plane)
        beyond = by_parity(from_near_ref[line, :], from_far_ref[line, :])
        f = 0.5 * (head(ROW_DHI) + jnp.where(wall, 0.0, beyond))
        inv = 1.0 / (g + f + leak_r)
        a = g * inv
        b = f * inv
        through = a * f
        b_cut = jnp.where(wall, 0.0, b)
        own_ref[OWN_A + plane : OWN_A + plane + 1, :] = a
        own_ref[OWN_B + plane : OWN_B + plane + 1, :] = b
        values[ROW_G + plane] = jnp.where(wall, 0.0, through)
        leak_l = head(ROW_EL) + a * leak_r
        values[ROW_EL + plane] = jnp.where(wall, leak_l + through, leak_l)
        values[ROW_ER + plane] = b_cut * leak_r
        ends = solve_x(read, me, count_x, plane)
        for comp in range(COMPS):
            k = comp * PLANES + plane
            low, high = ends[comp]

            def store(t, value):
                plane_ref[k, segment(t), :] = value

            unfold(low, high, cx_ref, tx_ref, qx_ref, qtx_ref, plane, comp, store)
            turned = jnp.transpose(natural(plane_ref, k))
            spread(turn_ref, k, turned)
            turn_ref[k, 0:1, :] = turned[0:1] + extra_ref[k : k + 1, :]
            final = PITCH * 7 + SEG - 1
            turn_ref[k, final : final + 1, :] = turned[LANES - 1 :] + extra_ref[8 + k : 9 + k, :]
            sources = [turn_ref[k, segment(t), :] for t in range(SEG)]
            left, right = condense(sources, cy_ref, ty_ref, q_ref, qtree_ref, plane, comp)
            right = right[0:1]
            own_ref[OWN_Q + k : OWN_Q + k + 1, :] = inv * right
            values[Y_JL + k] = left[0:1] + a * right
            values[Y_JR + k] = b_cut * right
    for which, value in values.items():
        send_row(out_ref, ROWS_Y, which, count_y, value)


def final_kernel(count, got_ref, own_ref, coef_ref, tree_ref, q_ref, qtree_ref, out_ref, plane_ref,
                 turn_ref, ring_ref, sem):
    me = lax.axis_index("gy")
    read = reader(got_ref, ring_ref, ROWS_Y, ORDER_Y, me)
    copies = []
    for plane in range(PLANES):
        ends = solve_y(read, own_ref, me, count, plane)
        for comp in range(COMPS):
            k = comp * PLANES + plane
            low, high = ends[comp]

            def store(t, value):
                plane_ref[k, segment(t), :] = value

            unfold(low, high, coef_ref, tree_ref, q_ref, qtree_ref, plane, comp, store)
            turn_ref[k] = jnp.transpose(natural(plane_ref, k))
            copy = pltpu.make_async_copy(turn_ref.at[k], out_ref.at[comp, plane], sem.at[k])
            copy.start()
            copies.append(copy)
    for copy in copies:
        copy.wait()


def shape(*dims):
    return jax.ShapeDtypeStruct(dims, f32)


def call(kernel, ins, outs, scratch, cost, *args):
    return pl.pallas_call(
        kernel,
        out_shape=tuple(o for o, _ in outs),
        in_specs=[pl.BlockSpec(memory_space=m) for m in ins],
        out_specs=tuple(pl.BlockSpec(memory_space=m) for _, m in outs),
        scratch_shapes=scratch,
        cost_estimate=pl.CostEstimate(flops=cost, bytes_accessed=1 << 19, transcendentals=0),
        compiler_params=pltpu.CompilerParams(vmem_limit_bytes=8 << 20),
    )(*args)


def share(sent, axis, order):
    pages = sent.reshape(len(order), -1, 2, LANES)
    got = lax.all_to_all(pages, axis, 0, 0, axis_index_groups=[order])
    return got.reshape(-1, LANES)


def local(velocity, diffusion):
    count_x = lax.axis_size("gx")
    count_y = lax.axis_size("gy")
    tile = (8, LANES)
    n = COMPS * PLANES
    low, high, near, far, cells, diff, turned = call(
        edges_kernel,
        (HBM, HBM),
        [
            (shape(*tile), VMEM),
            (shape(*tile), VMEM),
            (shape(*tile), VMEM),
            (shape(*tile), VMEM),
            (shape(COMPS, PLANES, LANES, LANES), VMEM),
            (shape(PLANES, LANES, LANES), VMEM),
            (shape(PLANES, LANES, LANES), VMEM),
        ],
        [pltpu.SemaphoreType.DMA((2,))],
        1 << 17,
        pltpu.with_memory_space_constraint(velocity, HBM),
        pltpu.with_memory_space_constraint(diffusion, HBM),
    )
    ring = range(count_y)
    from_far = lax.ppermute(far, "gy", [(i, (i - 1 + 2 * (i % 2)) % count_y) for i in ring])
    from_near = lax.ppermute(near, "gy", [(i, i ^ 1) for i in ring])
    coef = (shape(PLANES, 3, SEG, *tile), VMEM)
    tree = (shape(PLANES, 3, 3, *tile), VMEM)
    head = (shape(16, LANES), VMEM)
    q_all = (shape(n, SEG, *tile), VMEM)
    q_tree = (shape(n, 3, *tile), VMEM)
    block = VMEM((n, LANES, LANES), f32)
    pitched = VMEM((n, 8 * PITCH, LANES), f32)
    square = VMEM((LANES, LANES), f32)
    pair = VMEM((PLANES, LANES, LANES), f32)
    coef_pack = (shape(1, 3, SEG, *tile), VMEM)
    tree_pack = (shape(1, 3, 3, *tile), VMEM)
    cx, tx, hx, cy, ty, hy, cp, tp, vp = call(
        matrix_kernel,
        (VMEM,) * 4,
        [coef, tree, head] * 2 + [coef_pack, tree_pack, (shape(SEG, *tile), VMEM)],
        [pair, pair],
        1 << 21,
        diff, turned, low, high,
    )
    page, qx, qtx = call(
        source_kernel,
        (VMEM,) * 4,
        [(shape(40, LANES), VMEM), q_all, q_tree],
        [],
        1 << 22,
        cells, cx, tx, hx,
    )
    sent, qp, qtp = call(
        partial(halo_kernel, count_x),
        (VMEM,) * 6,
        [
            (shape(count_x * ROWS_X, LANES), VMEM),
            (shape(1, SEG, *tile), VMEM),
            (shape(1, 3, *tile), VMEM),
        ],
        [square, VMEM((1, 8 * PITCH, LANES), f32)],
        1 << 18,
        from_near, from_far, vp, cp, tp, page,
    )
    got = share(sent, "gx", ORDER_X)
    sent, qy, qty, own = call(
        partial(middle_kernel, count_x, count_y),
        (VMEM,) * 14,
        [(shape(count_y * ROWS_Y, LANES), VMEM), q_all, q_tree, head],
        [
            pitched,
            pitched,
            VMEM((1, 8 * PITCH, LANES), f32),
            square,
            VMEM((count_x * ROWS_X, LANES), f32),
        ],
        1 << 22,
        got, from_near, from_far, cx, tx, qx, qtx, cy, ty, hy, cp, tp, qp, qtp,
    )
    got = share(sent, "gy", ORDER_Y)
    (result,) = call(
        partial(final_kernel, count_y),
        (VMEM,) * 6,
        [(shape(COMPS, PLANES, LANES, LANES), HBM)],
        [
            pitched,
            block,
            VMEM((count_y * ROWS_Y, LANES), f32),
            pltpu.SemaphoreType.DMA((n,)),
        ],
        1 << 22,
        got, own, cy, ty, qy, qty,
    )
    return result


def solution(mesh):
    in_specs = (P(None, None, "gx", "gy"), P(None, "gx", "gy"))
    out_specs = P(None, None, "gx", "gy")
    return jax.shard_map(local, mesh=mesh, in_specs=in_specs, out_specs=out_specs, check_vma=False)
```

```python
from functools import partial

import jax
import jax.numpy as jnp
from jax import lax
from jax.experimental import pallas as pl
from jax.experimental.pallas import tpu as pltpu
from jax.sharding import PartitionSpec as P


COURANT = 0.25
HALF = 0.5 * COURANT
SEG = 16
PLANES = 2
COMPS = 3
LANES = 128
PITCH = 18
ROWS_X = 34
ROWS_Y = 18
ROW_G, ROW_EL, ROW_ER, ROW_DHI, ROW_VLO, ROW_DLO = 0, 2, 4, 6, 8, 14
ROW_JL, ROW_JR, ROW_VHI = 16, 22, 28
Y_JL, Y_JR = 6, 12
OWN_A, OWN_B, OWN_Q = 0, 2, 4

ORDER_X = [14, 3, 10, 8, 7, 0, 2, 15, 5, 4, 9, 11, 13, 12, 6, 1]
ORDER_Y = [13, 15, 1, 0, 3, 14, 6, 11, 2, 12, 7, 10, 8, 9, 4, 5]

f32 = jnp.float32
VMEM = pltpu.VMEM
HBM = pltpu.HBM


def sub_iota():
    return lax.broadcasted_iota(jnp.int32, (8, LANES), 0)


def lane_iota():
    return lax.broadcasted_iota(jnp.int32, (8, LANES), 1)


def ahead(x, count):
    return pltpu.roll(x, 8 - count, 0)


def after(x, count):
    return pltpu.roll(x, count, 0)


def strided(ref, lead, t):
    return ref[lead, pl.ds(t, 8, stride=SEG), :]


def segment(t):
    return pl.ds(t, 8, stride=PITCH)


def natural(ref, lead):
    starts = [PITCH * (i // 2) + 8 * (i % 2) for i in range(16)]
    return jnp.concatenate([ref[lead, start : start + 8, :] for start in starts], 0)


def spread(ref, lead, value):
    for i in range(16):
        start = PITCH * (i // 2) + 8 * (i % 2)
        ref[lead, start : start + 8, :] = value[8 * i : 8 * i + 8]


def factor(cells, first, coef_ref, tree_ref, head_ref, plane):
    row = sub_iota()
    last = row == 7
    faces = [0.5 * (cells[t] + cells[t + 1]) for t in range(SEG - 1)]
    faces.append(0.5 * (cells[SEG - 1] + ahead(cells[0], 1)))
    leak_l = 1.0 + jnp.where(jnp.logical_and(row == 0, first), 0.5 * cells[0], 0.0)
    g = faces[0]
    leak_r = jnp.ones_like(g)
    for t in range(1, SEG):
        f = faces[t]
        inv = 1.0 / (g + f + leak_r)
        a = g * inv
        b = f * inv
        if t == SEG - 1:
            inv = jnp.where(last, 0.0, inv)
            g = jnp.where(last, g, a * f)
            a = jnp.where(last, 0.0, a)
            b = jnp.where(last, 1.0, b)
            leak_l = leak_l + a * leak_r
            leak_r = b * leak_r
        else:
            g = a * f
            leak_l = leak_l + a * leak_r
            leak_r = 1.0 + b * leak_r
        coef_ref[plane, 0, t] = a
        coef_ref[plane, 1, t] = b
        coef_ref[plane, 2, t] = inv
    for level in range(3):
        count = 1 << level
        g_next = ahead(g, count)
        leak = leak_r + ahead(leak_l, count)
        inv = 1.0 / (g + g_next + leak)
        a = g * inv
        b = g_next * inv
        g = a * g_next
        leak_l = leak_l + a * leak
        leak_r = ahead(leak_r, count) + b * leak
        tree_ref[plane, level, 0] = a
        tree_ref[plane, level, 1] = b
        tree_ref[plane, level, 2] = inv
    if head_ref is None:
        return
    for base, value in ((ROW_G, g), (ROW_EL, leak_l), (ROW_ER, leak_r)):
        head_ref[base + plane : base + plane + 1, :] = value[0:1]
    head_ref[ROW_DHI + plane : ROW_DHI + plane + 1, :] = cells[SEG - 1][7:8]
    head_ref[ROW_DLO + plane : ROW_DLO + plane + 1, :] = cells[0][0:1]


def condense(sources, coef_ref, tree_ref, q_ref, qtree_ref, plane, comp):
    k = comp * PLANES + plane
    left = sources[0]
    right = sources[1]
    for t in range(1, SEG):
        q_ref[k, t] = coef_ref[plane, 2, t] * right
        left = left + coef_ref[plane, 0, t] * right
        right = coef_ref[plane, 1, t] * right
        if t < SEG - 1:
            right = right + sources[t + 1]
    for level in range(3):
        count = 1 << level
        j = right + ahead(left, count)
        left = left + tree_ref[plane, level, 0] * j
        right = ahead(right, count) + tree_ref[plane, level, 1] * j
        qtree_ref[k, level] = tree_ref[plane, level, 2] * j
    return left, right


def unfold(low, high, coef_ref, tree_ref, q_ref, qtree_ref, plane, comp, store):
    k = comp * PLANES + plane
    row = sub_iota()

    def mid(level, lo, hi):
        return (
            tree_ref[plane, level, 0] * lo
            + tree_ref[plane, level, 1] * hi
            + qtree_ref[k, level]
        )

    for level in (2, 1, 0):
        count = 1 << level
        between = mid(level, low, high)
        late = (row & count) != 0
        low = jnp.where(late, after(between, count), low)
        high = jnp.where(late, after(high, count), between)
    store(0, low)
    cell = high
    for t in range(SEG - 1, 0, -1):
        cell = (
            coef_ref[plane, 0, t] * low
            + q_ref[k, t]
            + coef_ref[plane, 1, t] * cell
        )
        store(t, cell)


def send_row(out_ref, rows, which, count, value):
    value = jnp.broadcast_to(value[0:1], (8, LANES))
    for half in range(count // 8):
        out_ref[pl.ds(8 * half * rows + which, 8, stride=rows), :] = value


def reader(got_ref, ring_ref, rows, order, me):
    count = len(order)
    for i, source in enumerate(order):
        base = ((source - me + count) & (count - 1)) * rows
        for start in range(0, rows, 8):
            size = min(8, rows - start)
            piece = got_ref[rows * i + start : rows * i + start + size, :]
            ring_ref[pl.ds(base + start, size), :] = piece

    def read(which):
        return tuple(
            ring_ref[pl.ds(8 * half * rows + which, 8, stride=rows), :] for half in (0, 1)
        )

    return read


def cyclic(me, half, count):
    return (me + 8 * half + sub_iota()) & (count - 1)


def solve_ring(blocks, me, count):
    halves = []
    for g, leak_l, leak_r, currents in blocks:
        levels = []
        for level in range(3):
            step = 1 << level
            g_next = ahead(g, step)
            leak = leak_r + ahead(leak_l, step)
            inv = 1.0 / (g + g_next + leak)
            a = g * inv
            b = g_next * inv
            g = a * g_next
            leak_l = leak_l + a * leak
            leak_r = ahead(leak_r, step) + b * leak
            levels.append((a, b, inv))
        merged = []
        for left, right in currents:
            terms = []
            for level in range(3):
                step = 1 << level
                a, b, inv = levels[level]
                j = right + ahead(left, step)
                left = left + a * j
                right = ahead(right, step) + b * j
                terms.append(inv * j)
            merged.append((left, right, terms))
        halves.append((g, leak_l, leak_r, levels, merged))
    g, leak_l, leak_r, levels, merged = halves[0]
    g_next, leak_l_next, leak_r_next, _, merged_next = halves[1]
    leak = leak_r + leak_l_next
    inv = 1.0 / (g + g_next + leak)
    a = g * inv
    b = g_next * inv
    total = 1.0 / (leak_l + a * leak + leak_r_next + b * leak)
    ends = []
    for comp in range(COMPS):
        left, right, terms = merged[comp]
        left_next, right_next, _ = merged_next[comp]
        j = right + left_next
        first = (left + a * j + right_next + b * j) * total
        high = (a + b) * first + inv * j
        for level in (2, 1, 0):
            high = levels[level][0] * first + levels[level][1] * high + terms[level]
        ends.append((first, jnp.where(me == count - 1, 0.0, high)))
    return ends


def solve_x(read, me, count, plane):
    row = sub_iota()

    def both(which):
        return read(which + plane)

    def before(pair, half):
        return jnp.where(row == 0, after(pair[1 - half], 1), after(pair[half], 1))

    def beyond(pair, half):
        return jnp.where(row == 7, ahead(pair[1 - half], 1), ahead(pair[half], 1))

    conduct = both(ROW_G)
    leaks_l = both(ROW_EL)
    leaks_r = both(ROW_ER)
    last_faces = both(ROW_DHI)
    first_faces = both(ROW_DLO)
    lefts = [both(ROW_JL + comp * PLANES) for comp in range(COMPS)]
    rights = [both(ROW_JR + comp * PLANES) for comp in range(COMPS)]
    low_cells = [both(ROW_VLO + comp * PLANES) for comp in range(COMPS)]
    high_cells = [both(ROW_VHI + comp * PLANES) for comp in range(COMPS)]
    blocks = []
    own = None
    for half in (0, 1):
        place = cyclic(me, half, count)
        wall = place == count - 1
        g = conduct[half]
        leak_l = leaks_l[half]
        leak_r = leaks_r[half]
        f = 0.5 * (last_faces[half] + jnp.where(wall, 0.0, beyond(first_faces, half)))
        inv = 1.0 / (g + f + leak_r)
        a = g * inv
        b = f * inv
        through = a * f
        leak_l = leak_l + a * leak_r
        leak_l = jnp.where(wall, leak_l + through, leak_l)
        up_lo = jnp.where(place == 0, 0.0, HALF * low_cells[0][half])
        up_hi = jnp.where(wall, 0.0, HALF * high_cells[0][half])
        b_cut = jnp.where(wall, 0.0, b)
        currents = []
        terms = []
        for comp in range(COMPS):
            left = lefts[comp][half] + up_lo * before(high_cells[comp], half)
            right = rights[comp][half] - up_hi * beyond(low_cells[comp], half)
            terms.append(inv * right)
            currents.append((left + a * right, b_cut * right))
        if half == 0:
            own = (a, b, terms)
        blocks.append((jnp.where(wall, 0.0, through), leak_l, b_cut * leak_r, currents))
    ends = solve_ring(blocks, me, count)
    a, b, terms = own
    return [
        (first, a * first + b * high + terms[comp]) for comp, (first, high) in enumerate(ends)
    ]


def solve_y(read, own_ref, me, count, plane):
    def own(which):
        return own_ref[which + plane : which + plane + 1, :]

    g, leak_l, leak_r = (read(which + plane) for which in (ROW_G, ROW_EL, ROW_ER))
    lefts = [read(Y_JL + comp * PLANES + plane) for comp in range(COMPS)]
    rights = [read(Y_JR + comp * PLANES + plane) for comp in range(COMPS)]
    blocks = [
        (
            g[half],
            leak_l[half],
            leak_r[half],
            [(lefts[comp][half], rights[comp][half]) for comp in range(COMPS)],
        )
        for half in (0, 1)
    ]
    ends = solve_ring(blocks, me, count)
    return [
        (first, own(OWN_A) * first + own(OWN_B) * high + own(OWN_Q + comp * PLANES))
        for comp, (first, high) in enumerate(ends)
    ]


def by_parity(even, odd):
    return jnp.where(lax.axis_index("gy") % 2 == 0, even, odd)


def edges_kernel(velocity_ref, diffusion_ref, low_ref, high_ref, near_ref, far_ref, v_ref, d_ref,
                 turn_ref, sem):
    copies = [
        pltpu.make_async_copy(velocity_ref, v_ref, sem.at[0]),
        pltpu.make_async_copy(diffusion_ref, d_ref, sem.at[1]),
    ]
    for copy in copies:
        copy.start()
    for copy in copies:
        copy.wait()
    for k in range(COMPS * PLANES + PLANES):
        if k < COMPS * PLANES:
            comp, plane = divmod(k, PLANES)
            turned = jnp.transpose(v_ref[comp, plane])
        else:
            turned = jnp.transpose(d_ref[k - 6])
            turn_ref[k - 6] = turned
        low = turned[0:1]
        high = turned[LANES - 1 : LANES]
        low_ref[k : k + 1, :] = low
        high_ref[k : k + 1, :] = high
        near_ref[k : k + 1, :] = by_parity(high, low)
        far_ref[k : k + 1, :] = by_parity(low, high)


def matrix_kernel(diffusion_ref, turn_ref, low_ref, high_ref, cx_ref, tx_ref, hx_ref, cy_ref, ty_ref,
                  hy_ref, cp_ref, tp_ref, vp_ref, edge_ref, pack_ref):
    first_x = lax.axis_index("gx") == 0
    first_y = lax.axis_index("gy") == 0
    edge_ref[...] = jnp.zeros((2, LANES, LANES), f32)
    for i, base in enumerate((2, 6)):
        for k in range(COMPS * PLANES):
            line = base + k % PLANES
            edge_ref[i, k : k + 1, :] = low_ref[line : line + 1, :]
            edge_ref[i, 8 + k : 9 + k, :] = high_ref[line : line + 1, :]
    for i in range(2):
        pack_ref[i] = jnp.transpose(edge_ref[i])
    for t in range(SEG):
        vp_ref[t] = strided(pack_ref, 0, t)
    for plane in range(PLANES):
        cells = [strided(diffusion_ref, plane, t) for t in range(SEG)]
        factor(cells, first_x, cx_ref, tx_ref, hx_ref, plane)
        cells = [strided(turn_ref, plane, t) for t in range(SEG)]
        factor(cells, first_y, cy_ref, ty_ref, hy_ref, plane)
    cells = [strided(pack_ref, 1, t) for t in range(SEG)]
    factor(cells, first_x, cp_ref, tp_ref, None, 0)
    for ref in (hx_ref, hy_ref):
        ref[ROW_VLO : ROW_VLO + 6, :] = jnp.zeros((6, LANES), f32)


def source_kernel(velocity_ref, coef_ref, tree_ref, head_ref, page_ref, q_ref, qtree_ref):
    row = sub_iota()
    lane = lane_iota()
    page_ref[0:16, :] = head_ref[...]
    page_ref[ROWS_X:, :] = jnp.zeros((40 - ROWS_X, LANES), f32)
    for plane in range(PLANES):
        cells = [
            [velocity_ref[comp, plane, pl.ds(t, 8, stride=SEG), :] for t in range(SEG)]
            for comp in range(COMPS)
        ]
        for comp in range(COMPS):
            k = comp * PLANES + plane
            own = cells[comp]
            sources = []
            for t in range(SEG):
                if t < SEG - 1:
                    fore = own[t + 1]
                else:
                    fore = jnp.where(row == 7, 0.0, ahead(own[0], 1))
                if t > 0:
                    back = own[t - 1]
                else:
                    back = jnp.where(row == 0, 0.0, after(own[SEG - 1], 1))
                right = jnp.where(lane == LANES - 1, 0.0, pltpu.roll(own[t], LANES - 1, 1))
                left = jnp.where(lane == 0, 0.0, pltpu.roll(own[t], 1, 1))
                sources.append(
                    own[t]
                    - HALF * (cells[0][t] * (fore - back) + cells[1][t] * (right - left))
                )
            left, right = condense(sources, coef_ref, tree_ref, q_ref, qtree_ref, plane, comp)
            page_ref[ROW_JL + k : ROW_JL + k + 1, :] = left[0:1]
            page_ref[ROW_JR + k : ROW_JR + k + 1, :] = right[0:1]
            page_ref[ROW_VLO + k : ROW_VLO + k + 1, :] = own[0][0:1]
            page_ref[ROW_VHI + k : ROW_VHI + k + 1, :] = own[SEG - 1][7:8]


def halo_kernel(count, from_near_ref, from_far_ref, vp_ref, coef_ref, tree_ref, page_ref, out_ref,
                q_ref, qtree_ref, edge_ref, halo_ref):
    me_y = lax.axis_index("gy")
    count_y = lax.axis_size("gy")
    row = sub_iota()
    lane = lane_iota()
    near = from_near_ref[...]
    far = from_far_ref[...]
    edge_ref[0:8, :] = jnp.where(me_y == 0, 0.0, HALF * by_parity(far, near))
    edge_ref[8:16, :] = jnp.where(me_y == count_y - 1, 0.0, -HALF * by_parity(near, far))
    edge_ref[16:, :] = jnp.zeros((LANES - 16, LANES), f32)
    spread(halo_ref, 0, jnp.transpose(edge_ref[...]))
    sources = [
        vp_ref[t] * halo_ref[0, segment(t), :]
        for t in range(SEG)
    ]
    ends = condense(sources, coef_ref, tree_ref, q_ref, qtree_ref, 0, 0)
    done = {}
    for base, value in zip((ROW_JL, ROW_JR), ends):
        value = jnp.broadcast_to(value[0:1], (8, LANES))
        low = jnp.sum(jnp.where(lane == row, value, 0.0), axis=1, keepdims=True)
        high = jnp.sum(jnp.where(lane == row + 8, value, 0.0), axis=1, keepdims=True)
        extra = jnp.where(lane == 0, low, jnp.where(lane == LANES - 1, high, 0.0))
        for k in range(COMPS * PLANES):
            done[base + k] = page_ref[base + k : base + k + 1, :] + extra[k : k + 1]
    for which in range(ROWS_X):
        value = done.get(which)
        if value is None:
            value = page_ref[which : which + 1, :]
        send_row(out_ref, ROWS_X, which, count, value)


def middle_kernel(count_x, count_y, got_ref, from_near_ref, from_far_ref, cx_ref, tx_ref, qx_ref, qtx_ref, cy_ref,
                  ty_ref, hy_ref, cp_ref, tp_ref, qp_ref, qtp_ref, out_ref, q_ref, qtree_ref, own_ref,
                  plane_ref, turn_ref, pack_ref, extra_ref, ring_ref):
    me = lax.axis_index("gx")

    def store_pack(t, value):
        pack_ref[0, segment(t), :] = value

    nothing = jnp.zeros((8, LANES), f32)
    unfold(nothing, nothing, cp_ref, tp_ref, qp_ref, qtp_ref, 0, 0, store_pack)
    extra_ref[...] = jnp.transpose(natural(pack_ref, 0))
    wall = lax.axis_index("gy") == count_y - 1
    read = reader(got_ref, ring_ref, ROWS_X, ORDER_X, me)
    own_ref[10:16, :] = jnp.zeros((6, LANES), f32)
    values = {}
    for plane in range(PLANES):

        def head(which):
            return hy_ref[which + plane : which + plane + 1, :]

        g = head(ROW_G)
        leak_r = head(ROW_ER)
        line = slice(6 + plane, 7 + plane)
        beyond = by_parity(from_near_ref[line, :], from_far_ref[line, :])
        f = 0.5 * (head(ROW_DHI) + jnp.where(wall, 0.0, beyond))
        inv = 1.0 / (g + f + leak_r)
        a = g * inv
        b = f * inv
        through = a * f
        b_cut = jnp.where(wall, 0.0, b)
        own_ref[OWN_A + plane : OWN_A + plane + 1, :] = a
        own_ref[OWN_B + plane : OWN_B + plane + 1, :] = b
        values[ROW_G + plane] = jnp.where(wall, 0.0, through)
        leak_l = head(ROW_EL) + a * leak_r
        values[ROW_EL + plane] = jnp.where(wall, leak_l + through, leak_l)
        values[ROW_ER + plane] = b_cut * leak_r
        ends = solve_x(read, me, count_x, plane)
        for comp in range(COMPS):
            k = comp * PLANES + plane
            low, high = ends[comp]

            def store(t, value):
                plane_ref[k, segment(t), :] = value

            unfold(low, high, cx_ref, tx_ref, qx_ref, qtx_ref, plane, comp, store)
            turned = jnp.transpose(natural(plane_ref, k))
            spread(turn_ref, k, turned)
            turn_ref[k, 0:1, :] = turned[0:1] + extra_ref[k : k + 1, :]
            final = PITCH * 7 + SEG - 1
            turn_ref[k, final : final + 1, :] = turned[LANES - 1 :] + extra_ref[8 + k : 9 + k, :]
            sources = [turn_ref[k, segment(t), :] for t in range(SEG)]
            left, right = condense(sources, cy_ref, ty_ref, q_ref, qtree_ref, plane, comp)
            right = right[0:1]
            own_ref[OWN_Q + k : OWN_Q + k + 1, :] = inv * right
            values[Y_JL + k] = left[0:1] + a * right
            values[Y_JR + k] = b_cut * right
    for which, value in values.items():
        send_row(out_ref, ROWS_Y, which, count_y, value)


def final_kernel(count, got_ref, own_ref, coef_ref, tree_ref, q_ref, qtree_ref, out_ref, plane_ref,
                 turn_ref, ring_ref, sem):
    me = lax.axis_index("gy")
    read = reader(got_ref, ring_ref, ROWS_Y, ORDER_Y, me)
    copies = []
    for plane in range(PLANES):
        ends = solve_y(read, own_ref, me, count, plane)
        for comp in range(COMPS):
            k = comp * PLANES + plane
            low, high = ends[comp]

            def store(t, value):
                plane_ref[k, segment(t), :] = value

            unfold(low, high, coef_ref, tree_ref, q_ref, qtree_ref, plane, comp, store)
            turn_ref[k] = jnp.transpose(natural(plane_ref, k))
            copy = pltpu.make_async_copy(turn_ref.at[k], out_ref.at[comp, plane], sem.at[k])
            copy.start()
            copies.append(copy)
    for copy in copies:
        copy.wait()


def shape(*dims):
    return jax.ShapeDtypeStruct(dims, f32)


def call(kernel, ins, outs, scratch, cost, *args):
    return pl.pallas_call(
        kernel,
        out_shape=tuple(o for o, _ in outs),
        in_specs=[pl.BlockSpec(memory_space=m) for m in ins],
        out_specs=tuple(pl.BlockSpec(memory_space=m) for _, m in outs),
        scratch_shapes=scratch,
        cost_estimate=pl.CostEstimate(flops=cost, bytes_accessed=1 << 19, transcendentals=0),
        compiler_params=pltpu.CompilerParams(vmem_limit_bytes=8 << 20),
    )(*args)


def share(sent, axis, order):
    pages = sent.reshape(len(order), -1, 2, LANES)
    got = lax.all_to_all(pages, axis, 0, 0, axis_index_groups=[order])
    return got.reshape(-1, LANES)


def local(velocity, diffusion):
    count_x = lax.axis_size("gx")
    count_y = lax.axis_size("gy")
    tile = (8, LANES)
    n = COMPS * PLANES
    low, high, near, far, cells, diff, turned = call(
        edges_kernel,
        (HBM, HBM),
        [
            (shape(*tile), VMEM),
            (shape(*tile), VMEM),
            (shape(*tile), VMEM),
            (shape(*tile), VMEM),
            (shape(COMPS, PLANES, LANES, LANES), VMEM),
            (shape(PLANES, LANES, LANES), VMEM),
            (shape(PLANES, LANES, LANES), VMEM),
        ],
        [pltpu.SemaphoreType.DMA((2,))],
        1 << 17,
        pltpu.with_memory_space_constraint(velocity, HBM),
        pltpu.with_memory_space_constraint(diffusion, HBM),
    )
    ring = range(count_y)
    from_far = lax.ppermute(far, "gy", [(i, (i - 1 + 2 * (i % 2)) % count_y) for i in ring])
    from_near = lax.ppermute(near, "gy", [(i, i ^ 1) for i in ring])
    coef = (shape(PLANES, 3, SEG, *tile), VMEM)
    tree = (shape(PLANES, 3, 3, *tile), VMEM)
    head = (shape(16, LANES), VMEM)
    q_all = (shape(n, SEG, *tile), VMEM)
    q_tree = (shape(n, 3, *tile), VMEM)
    block = VMEM((n, LANES, LANES), f32)
    pitched = VMEM((n, 8 * PITCH, LANES), f32)
    square = VMEM((LANES, LANES), f32)
    pair = VMEM((PLANES, LANES, LANES), f32)
    coef_pack = (shape(1, 3, SEG, *tile), VMEM)
    tree_pack = (shape(1, 3, 3, *tile), VMEM)
    cx, tx, hx, cy, ty, hy, cp, tp, vp = call(
        matrix_kernel,
        (VMEM,) * 4,
        [coef, tree, head] * 2 + [coef_pack, tree_pack, (shape(SEG, *tile), VMEM)],
        [pair, pair],
        1 << 21,
        diff, turned, low, high,
    )
    page, qx, qtx = call(
        source_kernel,
        (VMEM,) * 4,
        [(shape(40, LANES), VMEM), q_all, q_tree],
        [],
        1 << 22,
        cells, cx, tx, hx,
    )
    sent, qp, qtp = call(
        partial(halo_kernel, count_x),
        (VMEM,) * 6,
        [
            (shape(count_x * ROWS_X, LANES), VMEM),
            (shape(1, SEG, *tile), VMEM),
            (shape(1, 3, *tile), VMEM),
        ],
        [square, VMEM((1, 8 * PITCH, LANES), f32)],
        1 << 18,
        from_near, from_far, vp, cp, tp, page,
    )
    got = share(sent, "gx", ORDER_X)
    sent, qy, qty, own = call(
        partial(middle_kernel, count_x, count_y),
        (VMEM,) * 14,
        [(shape(count_y * ROWS_Y, LANES), VMEM), q_all, q_tree, head],
        [
            pitched,
            pitched,
            VMEM((1, 8 * PITCH, LANES), f32),
            square,
            VMEM((count_x * ROWS_X, LANES), f32),
        ],
        1 << 22,
        got, from_near, from_far, cx, tx, qx, qtx, cy, ty, hy, cp, tp, qp, qtp,
    )
    got = share(sent, "gy", ORDER_Y)
    (result,) = call(
        partial(final_kernel, count_y),
        (VMEM,) * 6,
        [(shape(COMPS, PLANES, LANES, LANES), HBM)],
        [
            pitched,
            block,
            VMEM((count_y * ROWS_Y, LANES), f32),
            pltpu.SemaphoreType.DMA((n,)),
        ],
        1 << 22,
        got, own, cy, ty, qy, qty,
    )
    return result


def solution(mesh):
    in_specs = (P(None, None, "gx", "gy"), P(None, "gx", "gy"))
    out_specs = P(None, None, "gx", "gy")
    return jax.shard_map(local, mesh=mesh, in_specs=in_specs, out_specs=out_specs, check_vma=False)
```

```python
from functools import partial

import jax
import jax.numpy as jnp
from jax import lax
from jax.experimental import pallas as pl
from jax.experimental.pallas import tpu as pltpu
from jax.sharding import PartitionSpec as P


COURANT = 0.25
HALF = 0.5 * COURANT
SEG = 16
PLANES = 2
COMPS = 3
LANES = 128
PITCH = 18
ROWS_X = 34
ROWS_Y = 18
ROW_G, ROW_EL, ROW_ER, ROW_DHI, ROW_VLO, ROW_DLO = 0, 2, 4, 6, 8, 14
ROW_JL, ROW_JR, ROW_VHI = 16, 22, 28
Y_JL, Y_JR = 6, 12
OWN_A, OWN_B, OWN_Q = 0, 2, 4

ORDER_X = [10, 12, 14, 3, 7, 1, 13, 15, 5, 8, 11, 6, 4, 9, 0, 2]
ORDER_Y = [13, 0, 1, 15, 3, 14, 6, 11, 2, 12, 7, 10, 8, 9, 4, 5]

f32 = jnp.float32
VMEM = pltpu.VMEM
HBM = pltpu.HBM


def sub_iota():
    return lax.broadcasted_iota(jnp.int32, (8, LANES), 0)


def lane_iota():
    return lax.broadcasted_iota(jnp.int32, (8, LANES), 1)


def ahead(x, count):
    return pltpu.roll(x, 8 - count, 0)


def after(x, count):
    return pltpu.roll(x, count, 0)


def strided(ref, lead, t):
    return ref[lead, pl.ds(t, 8, stride=SEG), :]


def segment(t):
    return pl.ds(t, 8, stride=PITCH)


def natural(ref, lead):
    starts = [PITCH * (i // 2) + 8 * (i % 2) for i in range(16)]
    return jnp.concatenate([ref[lead, start : start + 8, :] for start in starts], 0)


def spread(ref, lead, value):
    for i in range(16):
        start = PITCH * (i // 2) + 8 * (i % 2)
        ref[lead, start : start + 8, :] = value[8 * i : 8 * i + 8]


def factor(cells, first, coef_ref, tree_ref, head_ref, plane):
    row = sub_iota()
    last = row == 7
    faces = [0.5 * (cells[t] + cells[t + 1]) for t in range(SEG - 1)]
    faces.append(0.5 * (cells[SEG - 1] + ahead(cells[0], 1)))
    leak_l = 1.0 + jnp.where(jnp.logical_and(row == 0, first), 0.5 * cells[0], 0.0)
    g = faces[0]
    leak_r = jnp.ones_like(g)
    for t in range(1, SEG):
        f = faces[t]
        inv = 1.0 / (g + f + leak_r)
        a = g * inv
        b = f * inv
        if t == SEG - 1:
            inv = jnp.where(last, 0.0, inv)
            g = jnp.where(last, g, a * f)
            a = jnp.where(last, 0.0, a)
            b = jnp.where(last, 1.0, b)
            leak_l = leak_l + a * leak_r
            leak_r = b * leak_r
        else:
            g = a * f
            leak_l = leak_l + a * leak_r
            leak_r = 1.0 + b * leak_r
        coef_ref[plane, 0, t] = a
        coef_ref[plane, 1, t] = b
        coef_ref[plane, 2, t] = inv
    for level in range(3):
        count = 1 << level
        g_next = ahead(g, count)
        leak = leak_r + ahead(leak_l, count)
        inv = 1.0 / (g + g_next + leak)
        a = g * inv
        b = g_next * inv
        g = a * g_next
        leak_l = leak_l + a * leak
        leak_r = ahead(leak_r, count) + b * leak
        tree_ref[plane, level, 0] = a
        tree_ref[plane, level, 1] = b
        tree_ref[plane, level, 2] = inv
    if head_ref is None:
        return
    for base, value in ((ROW_G, g), (ROW_EL, leak_l), (ROW_ER, leak_r)):
        head_ref[base + plane : base + plane + 1, :] = value[0:1]
    head_ref[ROW_DHI + plane : ROW_DHI + plane + 1, :] = cells[SEG - 1][7:8]
    head_ref[ROW_DLO + plane : ROW_DLO + plane + 1, :] = cells[0][0:1]


def condense(sources, coef_ref, tree_ref, q_ref, qtree_ref, plane, comp):
    k = comp * PLANES + plane
    left = sources[0]
    right = sources[1]
    for t in range(1, SEG):
        q_ref[k, t] = coef_ref[plane, 2, t] * right
        left = left + coef_ref[plane, 0, t] * right
        right = coef_ref[plane, 1, t] * right
        if t < SEG - 1:
            right = right + sources[t + 1]
    for level in range(3):
        count = 1 << level
        j = right + ahead(left, count)
        left = left + tree_ref[plane, level, 0] * j
        right = ahead(right, count) + tree_ref[plane, level, 1] * j
        qtree_ref[k, level] = tree_ref[plane, level, 2] * j
    return left, right


def unfold(low, high, coef_ref, tree_ref, q_ref, qtree_ref, plane, comp, store):
    k = comp * PLANES + plane
    row = sub_iota()

    def mid(level, lo, hi):
        return (
            tree_ref[plane, level, 0] * lo
            + tree_ref[plane, level, 1] * hi
            + qtree_ref[k, level]
        )

    for level in (2, 1, 0):
        count = 1 << level
        between = mid(level, low, high)
        late = (row & count) != 0
        low = jnp.where(late, after(between, count), low)
        high = jnp.where(late, after(high, count), between)
    store(0, low)
    cell = high
    for t in range(SEG - 1, 0, -1):
        cell = (
            coef_ref[plane, 0, t] * low
            + q_ref[k, t]
            + coef_ref[plane, 1, t] * cell
        )
        store(t, cell)


def send_row(out_ref, rows, which, count, value):
    value = jnp.broadcast_to(value[0:1], (8, LANES))
    for half in range(count // 8):
        out_ref[pl.ds(8 * half * rows + which, 8, stride=rows), :] = value


def reader(got_ref, ring_ref, rows, order, me):
    count = len(order)
    for i, source in enumerate(order):
        base = ((source - me + count) & (count - 1)) * rows
        for start in range(0, rows, 8):
            size = min(8, rows - start)
            piece = got_ref[rows * i + start : rows * i + start + size, :]
            ring_ref[pl.ds(base + start, size), :] = piece

    def read(which):
        return tuple(
            ring_ref[pl.ds(8 * half * rows + which, 8, stride=rows), :] for half in (0, 1)
        )

    return read


def cyclic(me, half, count):
    return (me + 8 * half + sub_iota()) & (count - 1)


def solve_ring(blocks, me, count):
    halves = []
    for g, leak_l, leak_r, currents in blocks:
        levels = []
        for level in range(3):
            step = 1 << level
            g_next = ahead(g, step)
            leak = leak_r + ahead(leak_l, step)
            inv = 1.0 / (g + g_next + leak)
            a = g * inv
            b = g_next * inv
            g = a * g_next
            leak_l = leak_l + a * leak
            leak_r = ahead(leak_r, step) + b * leak
            levels.append((a, b, inv))
        merged = []
        for left, right in currents:
            terms = []
            for level in range(3):
                step = 1 << level
                a, b, inv = levels[level]
                j = right + ahead(left, step)
                left = left + a * j
                right = ahead(right, step) + b * j
                terms.append(inv * j)
            merged.append((left, right, terms))
        halves.append((g, leak_l, leak_r, levels, merged))
    g, leak_l, leak_r, levels, merged = halves[0]
    g_next, leak_l_next, leak_r_next, _, merged_next = halves[1]
    leak = leak_r + leak_l_next
    inv = 1.0 / (g + g_next + leak)
    a = g * inv
    b = g_next * inv
    total = 1.0 / (leak_l + a * leak + leak_r_next + b * leak)
    ends = []
    for comp in range(COMPS):
        left, right, terms = merged[comp]
        left_next, right_next, _ = merged_next[comp]
        j = right + left_next
        first = (left + a * j + right_next + b * j) * total
        high = (a + b) * first + inv * j
        for level in (2, 1, 0):
            high = levels[level][0] * first + levels[level][1] * high + terms[level]
        ends.append((first, jnp.where(me == count - 1, 0.0, high)))
    return ends


def solve_x(read, me, count, plane):
    row = sub_iota()

    def both(which):
        return read(which + plane)

    def before(pair, half):
        return jnp.where(row == 0, after(pair[1 - half], 1), after(pair[half], 1))

    def beyond(pair, half):
        return jnp.where(row == 7, ahead(pair[1 - half], 1), ahead(pair[half], 1))

    conduct = both(ROW_G)
    leaks_l = both(ROW_EL)
    leaks_r = both(ROW_ER)
    last_faces = both(ROW_DHI)
    first_faces = both(ROW_DLO)
    lefts = [both(ROW_JL + comp * PLANES) for comp in range(COMPS)]
    rights = [both(ROW_JR + comp * PLANES) for comp in range(COMPS)]
    low_cells = [both(ROW_VLO + comp * PLANES) for comp in range(COMPS)]
    high_cells = [both(ROW_VHI + comp * PLANES) for comp in range(COMPS)]
    blocks = []
    own = None
    for half in (0, 1):
        place = cyclic(me, half, count)
        wall = place == count - 1
        g = conduct[half]
        leak_l = leaks_l[half]
        leak_r = leaks_r[half]
        f = 0.5 * (last_faces[half] + jnp.where(wall, 0.0, beyond(first_faces, half)))
        inv = 1.0 / (g + f + leak_r)
        a = g * inv
        b = f * inv
        through = a * f
        leak_l = leak_l + a * leak_r
        leak_l = jnp.where(wall, leak_l + through, leak_l)
        up_lo = jnp.where(place == 0, 0.0, HALF * low_cells[0][half])
        up_hi = jnp.where(wall, 0.0, HALF * high_cells[0][half])
        b_cut = jnp.where(wall, 0.0, b)
        currents = []
        terms = []
        for comp in range(COMPS):
            left = lefts[comp][half] + up_lo * before(high_cells[comp], half)
            right = rights[comp][half] - up_hi * beyond(low_cells[comp], half)
            terms.append(inv * right)
            currents.append((left + a * right, b_cut * right))
        if half == 0:
            own = (a, b, terms)
        blocks.append((jnp.where(wall, 0.0, through), leak_l, b_cut * leak_r, currents))
    ends = solve_ring(blocks, me, count)
    a, b, terms = own
    return [
        (first, a * first + b * high + terms[comp]) for comp, (first, high) in enumerate(ends)
    ]


def solve_y(read, own_ref, me, count, plane):
    def own(which):
        return own_ref[which + plane : which + plane + 1, :]

    g, leak_l, leak_r = (read(which + plane) for which in (ROW_G, ROW_EL, ROW_ER))
    lefts = [read(Y_JL + comp * PLANES + plane) for comp in range(COMPS)]
    rights = [read(Y_JR + comp * PLANES + plane) for comp in range(COMPS)]
    blocks = [
        (
            g[half],
            leak_l[half],
            leak_r[half],
            [(lefts[comp][half], rights[comp][half]) for comp in range(COMPS)],
        )
        for half in (0, 1)
    ]
    ends = solve_ring(blocks, me, count)
    return [
        (first, own(OWN_A) * first + own(OWN_B) * high + own(OWN_Q + comp * PLANES))
        for comp, (first, high) in enumerate(ends)
    ]


def by_parity(even, odd):
    return jnp.where(lax.axis_index("gy") % 2 == 0, even, odd)


def edges_kernel(velocity_ref, diffusion_ref, low_ref, high_ref, near_ref, far_ref, v_ref, d_ref,
                 turn_ref, sem):
    copies = [
        pltpu.make_async_copy(velocity_ref, v_ref, sem.at[0]),
        pltpu.make_async_copy(diffusion_ref, d_ref, sem.at[1]),
    ]
    for copy in copies:
        copy.start()
    for copy in copies:
        copy.wait()
    for k in range(COMPS * PLANES + PLANES):
        if k < COMPS * PLANES:
            comp, plane = divmod(k, PLANES)
            turned = jnp.transpose(v_ref[comp, plane])
        else:
            turned = jnp.transpose(d_ref[k - 6])
            turn_ref[k - 6] = turned
        low = turned[0:1]
        high = turned[LANES - 1 : LANES]
        low_ref[k : k + 1, :] = low
        high_ref[k : k + 1, :] = high
        near_ref[k : k + 1, :] = by_parity(high, low)
        far_ref[k : k + 1, :] = by_parity(low, high)


def matrix_kernel(diffusion_ref, turn_ref, low_ref, high_ref, cx_ref, tx_ref, hx_ref, cy_ref, ty_ref,
                  hy_ref, cp_ref, tp_ref, vp_ref, edge_ref, pack_ref):
    first_x = lax.axis_index("gx") == 0
    first_y = lax.axis_index("gy") == 0
    edge_ref[...] = jnp.zeros((2, LANES, LANES), f32)
    for i, base in enumerate((2, 6)):
        for k in range(COMPS * PLANES):
            line = base + k % PLANES
            edge_ref[i, k : k + 1, :] = low_ref[line : line + 1, :]
            edge_ref[i, 8 + k : 9 + k, :] = high_ref[line : line + 1, :]
    for i in range(2):
        pack_ref[i] = jnp.transpose(edge_ref[i])
    for t in range(SEG):
        vp_ref[t] = strided(pack_ref, 0, t)
    for plane in range(PLANES):
        cells = [strided(diffusion_ref, plane, t) for t in range(SEG)]
        factor(cells, first_x, cx_ref, tx_ref, hx_ref, plane)
        cells = [strided(turn_ref, plane, t) for t in range(SEG)]
        factor(cells, first_y, cy_ref, ty_ref, hy_ref, plane)
    cells = [strided(pack_ref, 1, t) for t in range(SEG)]
    factor(cells, first_x, cp_ref, tp_ref, None, 0)
    for ref in (hx_ref, hy_ref):
        ref[ROW_VLO : ROW_VLO + 6, :] = jnp.zeros((6, LANES), f32)


def source_kernel(velocity_ref, coef_ref, tree_ref, head_ref, page_ref, q_ref, qtree_ref):
    row = sub_iota()
    lane = lane_iota()
    page_ref[0:16, :] = head_ref[...]
    page_ref[ROWS_X:, :] = jnp.zeros((40 - ROWS_X, LANES), f32)
    for plane in range(PLANES):
        cells = [
            [velocity_ref[comp, plane, pl.ds(t, 8, stride=SEG), :] for t in range(SEG)]
            for comp in range(COMPS)
        ]
        for comp in range(COMPS):
            k = comp * PLANES + plane
            own = cells[comp]
            sources = []
            for t in range(SEG):
                if t < SEG - 1:
                    fore = own[t + 1]
                else:
                    fore = jnp.where(row == 7, 0.0, ahead(own[0], 1))
                if t > 0:
                    back = own[t - 1]
                else:
                    back = jnp.where(row == 0, 0.0, after(own[SEG - 1], 1))
                right = jnp.where(lane == LANES - 1, 0.0, pltpu.roll(own[t], LANES - 1, 1))
                left = jnp.where(lane == 0, 0.0, pltpu.roll(own[t], 1, 1))
                sources.append(
                    own[t]
                    - HALF * (cells[0][t] * (fore - back) + cells[1][t] * (right - left))
                )
            left, right = condense(sources, coef_ref, tree_ref, q_ref, qtree_ref, plane, comp)
            page_ref[ROW_JL + k : ROW_JL + k + 1, :] = left[0:1]
            page_ref[ROW_JR + k : ROW_JR + k + 1, :] = right[0:1]
            page_ref[ROW_VLO + k : ROW_VLO + k + 1, :] = own[0][0:1]
            page_ref[ROW_VHI + k : ROW_VHI + k + 1, :] = own[SEG - 1][7:8]


def halo_kernel(count, from_near_ref, from_far_ref, vp_ref, coef_ref, tree_ref, page_ref, out_ref,
                q_ref, qtree_ref, edge_ref, halo_ref):
    me_y = lax.axis_index("gy")
    count_y = lax.axis_size("gy")
    row = sub_iota()
    lane = lane_iota()
    near = from_near_ref[...]
    far = from_far_ref[...]
    edge_ref[0:8, :] = jnp.where(me_y == 0, 0.0, HALF * by_parity(far, near))
    edge_ref[8:16, :] = jnp.where(me_y == count_y - 1, 0.0, -HALF * by_parity(near, far))
    edge_ref[16:, :] = jnp.zeros((LANES - 16, LANES), f32)
    spread(halo_ref, 0, jnp.transpose(edge_ref[...]))
    sources = [
        vp_ref[t] * halo_ref[0, segment(t), :]
        for t in range(SEG)
    ]
    ends = condense(sources, coef_ref, tree_ref, q_ref, qtree_ref, 0, 0)
    done = {}
    for base, value in zip((ROW_JL, ROW_JR), ends):
        value = jnp.broadcast_to(value[0:1], (8, LANES))
        low = jnp.sum(jnp.where(lane == row, value, 0.0), axis=1, keepdims=True)
        high = jnp.sum(jnp.where(lane == row + 8, value, 0.0), axis=1, keepdims=True)
        extra = jnp.where(lane == 0, low, jnp.where(lane == LANES - 1, high, 0.0))
        for k in range(COMPS * PLANES):
            done[base + k] = page_ref[base + k : base + k + 1, :] + extra[k : k + 1]
    for which in range(ROWS_X):
        value = done.get(which)
        if value is None:
            value = page_ref[which : which + 1, :]
        send_row(out_ref, ROWS_X, which, count, value)


def middle_kernel(count_x, count_y, got_ref, from_near_ref, from_far_ref, cx_ref, tx_ref, qx_ref, qtx_ref, cy_ref,
                  ty_ref, hy_ref, cp_ref, tp_ref, qp_ref, qtp_ref, out_ref, q_ref, qtree_ref, own_ref,
                  plane_ref, turn_ref, pack_ref, extra_ref, ring_ref):
    me = lax.axis_index("gx")

    def store_pack(t, value):
        pack_ref[0, segment(t), :] = value

    nothing = jnp.zeros((8, LANES), f32)
    unfold(nothing, nothing, cp_ref, tp_ref, qp_ref, qtp_ref, 0, 0, store_pack)
    extra_ref[...] = jnp.transpose(natural(pack_ref, 0))
    wall = lax.axis_index("gy") == count_y - 1
    read = reader(got_ref, ring_ref, ROWS_X, ORDER_X, me)
    own_ref[10:16, :] = jnp.zeros((6, LANES), f32)
    values = {}
    for plane in range(PLANES):

        def head(which):
            return hy_ref[which + plane : which + plane + 1, :]

        g = head(ROW_G)
        leak_r = head(ROW_ER)
        line = slice(6 + plane, 7 + plane)
        beyond = by_parity(from_near_ref[line, :], from_far_ref[line, :])
        f = 0.5 * (head(ROW_DHI) + jnp.where(wall, 0.0, beyond))
        inv = 1.0 / (g + f + leak_r)
        a = g * inv
        b = f * inv
        through = a * f
        b_cut = jnp.where(wall, 0.0, b)
        own_ref[OWN_A + plane : OWN_A + plane + 1, :] = a
        own_ref[OWN_B + plane : OWN_B + plane + 1, :] = b
        values[ROW_G + plane] = jnp.where(wall, 0.0, through)
        leak_l = head(ROW_EL) + a * leak_r
        values[ROW_EL + plane] = jnp.where(wall, leak_l + through, leak_l)
        values[ROW_ER + plane] = b_cut * leak_r
        ends = solve_x(read, me, count_x, plane)
        for comp in range(COMPS):
            k = comp * PLANES + plane
            low, high = ends[comp]

            def store(t, value):
                plane_ref[k, segment(t), :] = value

            unfold(low, high, cx_ref, tx_ref, qx_ref, qtx_ref, plane, comp, store)
            turned = jnp.transpose(natural(plane_ref, k))
            spread(turn_ref, k, turned)
            turn_ref[k, 0:1, :] = turned[0:1] + extra_ref[k : k + 1, :]
            final = PITCH * 7 + SEG - 1
            turn_ref[k, final : final + 1, :] = turned[LANES - 1 :] + extra_ref[8 + k : 9 + k, :]
            sources = [turn_ref[k, segment(t), :] for t in range(SEG)]
            left, right = condense(sources, cy_ref, ty_ref, q_ref, qtree_ref, plane, comp)
            right = right[0:1]
            own_ref[OWN_Q + k : OWN_Q + k + 1, :] = inv * right
            values[Y_JL + k] = left[0:1] + a * right
            values[Y_JR + k] = b_cut * right
    for which, value in values.items():
        send_row(out_ref, ROWS_Y, which, count_y, value)


def final_kernel(count, got_ref, own_ref, coef_ref, tree_ref, q_ref, qtree_ref, out_ref, plane_ref,
                 turn_ref, ring_ref, sem):
    me = lax.axis_index("gy")
    read = reader(got_ref, ring_ref, ROWS_Y, ORDER_Y, me)
    copies = []
    for plane in range(PLANES):
        ends = solve_y(read, own_ref, me, count, plane)
        for comp in range(COMPS):
            k = comp * PLANES + plane
            low, high = ends[comp]

            def store(t, value):
                plane_ref[k, segment(t), :] = value

            unfold(low, high, coef_ref, tree_ref, q_ref, qtree_ref, plane, comp, store)
            turn_ref[k] = jnp.transpose(natural(plane_ref, k))
            copy = pltpu.make_async_copy(turn_ref.at[k], out_ref.at[comp, plane], sem.at[k])
            copy.start()
            copies.append(copy)
    for copy in copies:
        copy.wait()


def shape(*dims):
    return jax.ShapeDtypeStruct(dims, f32)


def call(kernel, ins, outs, scratch, cost, *args):
    return pl.pallas_call(
        kernel,
        out_shape=tuple(o for o, _ in outs),
        in_specs=[pl.BlockSpec(memory_space=m) for m in ins],
        out_specs=tuple(pl.BlockSpec(memory_space=m) for _, m in outs),
        scratch_shapes=scratch,
        cost_estimate=pl.CostEstimate(flops=cost, bytes_accessed=1 << 19, transcendentals=0),
        compiler_params=pltpu.CompilerParams(vmem_limit_bytes=8 << 20),
    )(*args)


def share(sent, axis, order):
    pages = sent.reshape(len(order), -1, 2, LANES)
    got = lax.all_to_all(pages, axis, 0, 0, axis_index_groups=[order])
    return got.reshape(-1, LANES)


def local(velocity, diffusion):
    count_x = lax.axis_size("gx")
    count_y = lax.axis_size("gy")
    tile = (8, LANES)
    n = COMPS * PLANES
    low, high, near, far, cells, diff, turned = call(
        edges_kernel,
        (HBM, HBM),
        [
            (shape(*tile), VMEM),
            (shape(*tile), VMEM),
            (shape(*tile), VMEM),
            (shape(*tile), VMEM),
            (shape(COMPS, PLANES, LANES, LANES), VMEM),
            (shape(PLANES, LANES, LANES), VMEM),
            (shape(PLANES, LANES, LANES), VMEM),
        ],
        [pltpu.SemaphoreType.DMA((2,))],
        1 << 17,
        pltpu.with_memory_space_constraint(velocity, HBM),
        pltpu.with_memory_space_constraint(diffusion, HBM),
    )
    ring = range(count_y)
    from_far = lax.ppermute(far, "gy", [(i, (i - 1 + 2 * (i % 2)) % count_y) for i in ring])
    from_near = lax.ppermute(near, "gy", [(i, i ^ 1) for i in ring])
    coef = (shape(PLANES, 3, SEG, *tile), VMEM)
    tree = (shape(PLANES, 3, 3, *tile), VMEM)
    head = (shape(16, LANES), VMEM)
    q_all = (shape(n, SEG, *tile), VMEM)
    q_tree = (shape(n, 3, *tile), VMEM)
    block = VMEM((n, LANES, LANES), f32)
    pitched = VMEM((n, 8 * PITCH, LANES), f32)
    square = VMEM((LANES, LANES), f32)
    pair = VMEM((PLANES, LANES, LANES), f32)
    coef_pack = (shape(1, 3, SEG, *tile), VMEM)
    tree_pack = (shape(1, 3, 3, *tile), VMEM)
    cx, tx, hx, cy, ty, hy, cp, tp, vp = call(
        matrix_kernel,
        (VMEM,) * 4,
        [coef, tree, head] * 2 + [coef_pack, tree_pack, (shape(SEG, *tile), VMEM)],
        [pair, pair],
        1 << 21,
        diff, turned, low, high,
    )
    page, qx, qtx = call(
        source_kernel,
        (VMEM,) * 4,
        [(shape(40, LANES), VMEM), q_all, q_tree],
        [],
        1 << 22,
        cells, cx, tx, hx,
    )
    sent, qp, qtp = call(
        partial(halo_kernel, count_x),
        (VMEM,) * 6,
        [
            (shape(count_x * ROWS_X, LANES), VMEM),
            (shape(1, SEG, *tile), VMEM),
            (shape(1, 3, *tile), VMEM),
        ],
        [square, VMEM((1, 8 * PITCH, LANES), f32)],
        1 << 18,
        from_near, from_far, vp, cp, tp, page,
    )
    got = share(sent, "gx", ORDER_X)
    sent, qy, qty, own = call(
        partial(middle_kernel, count_x, count_y),
        (VMEM,) * 14,
        [(shape(count_y * ROWS_Y, LANES), VMEM), q_all, q_tree, head],
        [
            pitched,
            pitched,
            VMEM((1, 8 * PITCH, LANES), f32),
            square,
            VMEM((count_x * ROWS_X, LANES), f32),
        ],
        1 << 22,
        got, from_near, from_far, cx, tx, qx, qtx, cy, ty, hy, cp, tp, qp, qtp,
    )
    got = share(sent, "gy", ORDER_Y)
    (result,) = call(
        partial(final_kernel, count_y),
        (VMEM,) * 6,
        [(shape(COMPS, PLANES, LANES, LANES), HBM)],
        [
            pitched,
            block,
            VMEM((count_y * ROWS_Y, LANES), f32),
            pltpu.SemaphoreType.DMA((n,)),
        ],
        1 << 22,
        got, own, cy, ty, qy, qty,
    )
    return result


def solution(mesh):
    in_specs = (P(None, None, "gx", "gy"), P(None, "gx", "gy"))
    out_specs = P(None, None, "gx", "gy")
    return jax.shard_map(local, mesh=mesh, in_specs=in_specs, out_specs=out_specs, check_vma=False)
```
